256 devices in a mesh: wide: 16 (over y_hi, x, core), narrow: 16 (over z, y_lo).
Axes of the slice: x: 4, y: 4 (y_hi: 2, y_lo: 2; y = y_hi * 2 + y_lo), z: 8, core: 2. Of those that a mesh axis runs over, the one named last changes fastest.
Arguments:
- documents: bfloat16 [16384, 768], P('wide'), may hold values from -8 to 8
- label_weight: bfloat16 [32768, 768], P(('wide', 'narrow')), may hold values from -1 to 1
- sample_ids: int32 [32768], P(('wide', 'narrow')), may hold values from 0 to 2812280, as said below
- positive_cols: int32 [16384, 4], P('wide'), may hold values from 0 to 32767
- up_weight: bfloat16 [768, 3072], P(None, 'narrow'), may hold values from -0.21875 to 0.21875
- down_weight: bfloat16 [3072, 768], P('narrow'), may hold values from -0.109375 to 0.109375
Outputs:
- label_grad: float32 [32768, 768], P(('wide', 'narrow'))
- up_grad: float32 [768, 3072], P('wide', 'narrow')
- down_grad: float32 [3072, 768], P('narrow', 'wide')
The draws below stay inside these ranges and needn't reach their ends.
Inputs may be any that keep to these rules, and one draw needn't show every extreme that they name: `sample_ids`: frequency ranks (0 is the most frequent of 2812281 labels), not falling along the sampled columns; frequent ranks repeat.
All inputs are finite; a program needn't handle non-finite values.
Results may differ from the reference program's by a relative error of at most 0.01.
Values may be sent and summed in bfloat16 or wider, within the bound.
No kernel may reach another device: no remote copies, remote signals or barrier semaphores. Data moves between devices by JAX's collectives and lax.ppermute only.
A program may use at most 64 MiB of HBM per device.

```python
import math
from functools import partial
import jax
import jax.numpy as jnp
from jax import lax

D = 768
FF = 3072
CATALOG = 2812281
POS_DOC = 4
DOC_DEV = 1024
B = 16384
S = 32768


def rank_draw(key):
    key_expo, key_rank = jax.random.split(jax.random.fold_in(key, 5113))
    expo = jax.random.randint(key_expo, (S,), 0, 23)
    raw = jax.random.randint(key_rank, (S,), 0, jnp.left_shift(jnp.int32(1), expo))
    return jnp.sort(jnp.minimum(raw, CATALOG - 1))


def expected_log_drawn(rank_ids):
    rank_float = rank_ids.astype(jnp.float32)
    return jnp.log(jnp.float32(S)) + jnp.log(jnp.log1p(1.0 / (rank_float + 1.0))) - jnp.log(jnp.log(jnp.float32(CATALOG) + 1.0))


def draw_sample_ids(key, part):
    return rank_draw(key)


def draw_documents(key, part):
    key_base, key_scale = jax.random.split(jax.random.fold_in(key, 1201))
    base = jnp.clip(jax.random.normal(key_base, (B, D), jnp.float32), -4.0, 4.0)
    row_scale = jnp.exp(jax.random.uniform(key_scale, (B, 1), jnp.float32, math.log(0.5), math.log(2.0)))
    values = base * row_scale
    values = values.at[:, 0].set(8.0)
    return values.astype(jnp.bfloat16)


def draw_label_weight(key, part):
    key_base, key_scale = jax.random.split(jax.random.fold_in(key, 3307))
    base = jnp.clip(jax.random.normal(key_base, (S, D), jnp.float32), -4.0, 4.0)
    row_scale = jnp.exp(jax.random.uniform(key_scale, (S, 1), jnp.float32, math.log(0.5), math.log(2.0)))
    weights = base * row_scale * (1.5 / math.sqrt(D))
    first_column = jnp.clip(expected_log_drawn(rank_draw(key)) / 8.0, -1.0, 1.0)
    weights = weights.at[:, 0].set(first_column)
    return weights.astype(jnp.bfloat16)


def set_ends(values, rng, smallest, top_value):
    longest = values.shape.index(max(values.shape))
    spots = []
    for shift in (0, 1):
        where = [jax.random.randint(jax.random.fold_in(rng, axis), (), 0, length) for axis, length in enumerate(values.shape)]
        where[longest] = (where[longest] + shift) % values.shape[longest]
        spots.append(tuple(where))
    return values.at[spots[0]].set(smallest).at[spots[1]].set(top_value)


def levels(own_key, dims, cuts, smallest, high):
    loudness, own = 1.0, jax.random.fold_in(own_key, 6)
    for position, blocks in cuts:
        heights = jnp.exp(jax.random.uniform(jax.random.fold_in(own, position), (blocks,), jnp.float32, smallest / len(cuts), high / len(cuts)))
        loudness = loudness * jnp.repeat(heights, dims[position] // blocks).reshape([-1 if axis == position else 1 for axis in range(len(dims))])
    return loudness


def bell_draw(key, shape, width, bound, shards=(), kind=jnp.bfloat16):
    result = jax.random.normal(key, shape, jnp.float32) * width
    if len(shards) > 0:
        result = levels(key, shape, shards, -0.22, 0.18) * result
    return jnp.clip(result, min=-bound, max=bound).astype(kind)


def setup_inputs(seed: int = 0) -> dict:
    key_of = jax.random.split(jax.random.key(seed), 7)
    documents = draw_documents(jax.random.fold_in(key_of[6], 71), 0)
    label_weight = draw_label_weight(jax.random.fold_in(key_of[6], 71), 0)
    sample_ids = draw_sample_ids(jax.random.fold_in(key_of[6], 71), 0)
    positive_cols = set_ends(jax.random.randint(key_of[3], (B, POS_DOC), 0, S), jax.random.fold_in(key_of[3], 1), 0, S - 1).astype(jnp.int32)
    up_weight = bell_draw(key_of[4], (D, FF), D ** -0.5, 0.21875, ((1, 16),))
    down_weight = bell_draw(key_of[5], (FF, D), FF ** -0.5, 0.109375, ((0, 16),))
    return {"documents": documents, "label_weight": label_weight, "sample_ids": sample_ids, "positive_cols": positive_cols, "up_weight": up_weight, "down_weight": down_weight}


def expected_log(rank_ids, sampled):
    rank_float = rank_ids.astype(jnp.float32)
    return jnp.log(jnp.float32(sampled)) + jnp.log(jnp.log1p(1.0 / (rank_float + 1.0))) - jnp.log(jnp.log(jnp.float32(CATALOG) + 1.0))

def reference(documents, label_weight, sample_ids, positive_cols, up_weight, down_weight):
    log_expect = expected_log(sample_ids, S)
    pre_act = jnp.dot(documents, up_weight, preferred_element_type=jnp.float32)
    hidden = jax.nn.gelu(pre_act, approximate=False).astype(jnp.bfloat16)
    summed = jnp.dot(hidden, down_weight, preferred_element_type=jnp.float32)
    embedding = (documents.astype(jnp.float32) + summed).astype(jnp.bfloat16)
    groups = B // DOC_DEV
    doc_blocks = embedding.reshape(groups, DOC_DEV, D)
    pos_blocks = positive_cols.reshape(groups, DOC_DEV, POS_DOC)
    row_index = jnp.arange(DOC_DEV, dtype=jnp.int32)[:, None]

    def one_group(label_acc, block_item):
        doc_block, pos_block = block_item
        logits = jnp.dot(doc_block, label_weight.T, preferred_element_type=jnp.float32) - log_expect[None, :]
        row_top = lax.optimization_barrier(jnp.max(logits, axis=1, keepdims=True))
        log_total = row_top + jnp.log(lax.optimization_barrier(jnp.sum(jnp.exp(logits - row_top), axis=1, keepdims=True)))
        positive_hits = jnp.zeros(logits.shape, jnp.float32).at[row_index, pos_block].add(1.0)
        grad_logits = (jnp.exp(logits - log_total) - positive_hits / POS_DOC).astype(jnp.bfloat16)
        embed_back = jnp.dot(grad_logits, label_weight, preferred_element_type=jnp.float32)
        label_acc = label_acc + jnp.dot(grad_logits.T, doc_block, preferred_element_type=jnp.float32)
        return (label_acc, embed_back)
    label_grad, embed_back = lax.scan(one_group, jnp.zeros((S, D), jnp.float32), (doc_blocks, pos_blocks))
    embed_grad = embed_back.reshape(B, D).astype(jnp.bfloat16)
    act_grad = jnp.dot(embed_grad, down_weight.T, preferred_element_type=jnp.float32)
    _, gelu_pull = jax.vjp(partial(jax.nn.gelu, approximate=False), pre_act)
    pre_grad = gelu_pull(act_grad)[0].astype(jnp.bfloat16)
    down_grad = jnp.dot(hidden.T, embed_grad, preferred_element_type=jnp.float32)
    up_grad = jnp.dot(documents.T, pre_grad, preferred_element_type=jnp.float32)
    return (label_grad, up_grad, down_grad)
```

```python
from functools import partial

import jax
import jax.numpy as jnp
import numpy as np
from jax import lax
from jax.experimental import pallas as pl
from jax.experimental.pallas import tpu as pltpu
from jax.sharding import Mesh
from jax.sharding import PartitionSpec as P

CATALOG = 2812281
BF16, F32, I32 = jnp.bfloat16, jnp.float32, jnp.int32
D = 768
LAB = 128
EXTRA = 8
BLK = LAB + EXTRA
NB = 32
GRP = 4
TILE = GRP * LAB
STEPS = NB // GRP
DOCS = 512
REL = (0, -1, 1, 2)
NT = (((1,), (1,)), ((), ()))
TN = (((0,), (0,)), ((), ()))


def move(block, axes, size, distance):
    return lax.ppermute(block, axes, [(i, (i + distance) % size) for i in range(size)])


def gather_ring(block, axes, half):
    from_low = move(block, axes, 4, 1)
    from_high = move(block, axes, 4, -1)
    far_a = move(from_low[:half], axes, 4, 1)
    far_b = move(from_high[half:], axes, 4, -1)
    return jnp.concatenate([block, from_low, from_high, far_a, far_b], axis=0)


def add(a, b):
    return a.astype(F32) + b.astype(F32)


def scatter_ring(parts, axes, half):
    low_a = move(parts[3, :half], axes, 4, 1)
    high_b = move(parts[3, half:], axes, 4, -1)
    up = jnp.concatenate([add(parts[2, :half], low_a).astype(BF16), parts[2, half:]], axis=0)
    down = jnp.concatenate([parts[1, :half], add(parts[1, half:], high_b).astype(BF16)], axis=0)
    from_low = move(up, axes, 4, 1)
    from_high = move(down, axes, 4, -1)
    return add(parts[0], from_low) + from_high.astype(F32)


def total(parts):
    result = parts[0].astype(F32)
    for j in range(1, parts.shape[0]):
        result = result + parts[j].astype(F32)
    return result


def rounded(values):
    return lax.reduce_precision(values, 8, 7)


def log_expected(rank_ids, sampled):
    rank_float = rank_ids.astype(F32)
    return (
        jnp.log(F32(sampled))
        + jnp.log(jnp.log1p(1.0 / (rank_float + 1.0)))
        - jnp.log(jnp.log(F32(CATALOG) + 1.0))
    )


def take_rows(near_ref, far_ref, rows_ref):
    step = pl.program_id(0)

    @pl.when(step < STEPS // 2)
    def _():
        for j in range(GRP):
            rows_ref[j * LAB : (j + 1) * LAB, :] = near_ref[j, :LAB, :]

    @pl.when(step >= STEPS // 2)
    def _():
        for j in range(GRP):
            rows_ref[j * LAB : (j + 1) * LAB, :] = far_ref[j, :LAB, :]


def first_kernel(near_ref, far_ref, emb_ref, exp_ref, top_ref, stat_ref, rows, bias, run_max, run_sum):
    step = pl.program_id(0)
    take_rows(near_ref, far_ref, rows)

    @pl.when(step == 0)
    def _():
        run_max[...] = jnp.full_like(run_max, -jnp.inf)
        run_sum[...] = jnp.zeros_like(run_sum)

    def set_bias(ref):
        for j in range(GRP):
            pieces = ref[j, LAB:, :LAB].astype(F32)
            row = pieces[0:1] + pieces[1:2] + pieces[2:3]
            bias[j * LAB : (j + 1) * LAB, :] = jnp.broadcast_to(row, (LAB, LAB)).T

    @pl.when(step < STEPS // 2)
    def _():
        set_bias(near_ref)

    @pl.when(step >= STEPS // 2)
    def _():
        set_bias(far_ref)

    half = DOCS // 2
    for h in range(2):
        cols = slice(h * half, (h + 1) * half)
        raw = lax.dot_general(rows[...], emb_ref[cols, :], NT, preferred_element_type=F32)
        shift = jnp.concatenate([bias[...]] * (half // LAB), axis=1)
        logits = raw - shift
        old = run_max[:, cols]
        new = jnp.maximum(old, jnp.max(logits, axis=0, keepdims=True))
        exps = jnp.exp(logits - new)
        exp_ref[:, cols] = exps
        run_sum[:, cols] = run_sum[:, cols] * jnp.exp(old - new) + jnp.sum(exps, axis=0, keepdims=True)
        run_max[:, cols] = new
    top_ref[0] = run_max[...]

    @pl.when(step == STEPS - 1)
    def _():
        for j in range(4):
            stat_ref[j : j + 1, :] = run_max[:, j * 128 : (j + 1) * 128]
            stat_ref[4 + j : 5 + j, :] = run_sum[:, j * 128 : (j + 1) * 128]


def second_kernel(base_ref, near_ref, far_ref, exp_ref, top_ref, total_ref, pos_ref, grad_ref, out_ref, rows, acc):
    step = pl.program_id(0)
    take_rows(near_ref, far_ref, rows)

    @pl.when(step == 0)
    def _():
        acc[...] = jnp.zeros_like(acc)

    scale = jnp.exp(top_ref[0] - total_ref[...])
    for j in range(GRP):
        span = slice(j * LAB, (j + 1) * LAB)
        ids = base_ref[step * GRP + j] + lax.broadcasted_iota(I32, (LAB, DOCS), 0)
        hits = jnp.zeros((LAB, DOCS), F32)
        for k in range(4):
            hits = hits + jnp.where(pos_ref[k : k + 1, :] == ids, F32(0.25), F32(0.0))
        grad_ref[span, :] = (exp_ref[span, :] * scale - hits).astype(BF16)
    acc[...] += lax.dot_general(grad_ref[...], rows[...], TN, preferred_element_type=F32)

    @pl.when(step == STEPS - 1)
    def _():
        out_ref[...] = acc[...].astype(BF16)


def near_map(step, *_):
    return (jnp.minimum(step, STEPS // 2 - 1), 0, 0)


def far_map(step, *_):
    return (jnp.maximum(step - STEPS // 2, 0), 0, 0)


def first_pass(near, far, embedding):
    return pl.pallas_call(
        first_kernel,
        out_shape=(
            jax.ShapeDtypeStruct((NB * LAB, DOCS), F32),
            jax.ShapeDtypeStruct((STEPS, 1, DOCS), F32),
            jax.ShapeDtypeStruct((8, 128), F32),
        ),
        grid=(STEPS,),
        in_specs=[
            pl.BlockSpec((GRP, BLK, D), near_map),
            pl.BlockSpec((GRP, BLK, D), far_map),
            pl.BlockSpec((DOCS, D), lambda s: (0, 0)),
        ],
        out_specs=(
            pl.BlockSpec((TILE, DOCS), lambda s: (s, 0)),
            pl.BlockSpec((1, 1, DOCS), lambda s: (s, 0, 0)),
            pl.BlockSpec((8, 128), lambda s: (0, 0)),
        ),
        scratch_shapes=[
            pltpu.VMEM((TILE, D), BF16),
            pltpu.VMEM((TILE, LAB), F32),
            pltpu.VMEM((1, DOCS), F32),
            pltpu.VMEM((1, DOCS), F32),
        ],
        compiler_params=pltpu.CompilerParams(
            dimension_semantics=("arbitrary",), vmem_limit_bytes=40 << 20
        ),
        cost_estimate=pl.CostEstimate(
            flops=2 * NB * LAB * DOCS * D, bytes_accessed=16 << 20, transcendentals=NB * LAB * DOCS
        ),
        name="first_pass",
    )(near, far, embedding)


def second_pass(bases, near, far, exps, tops, log_total, positives):
    return pl.pallas_call(
        second_kernel,
        out_shape=(
            jax.ShapeDtypeStruct((NB * LAB, DOCS), BF16),
            jax.ShapeDtypeStruct((DOCS, D), BF16),
        ),
        grid_spec=pltpu.PrefetchScalarGridSpec(
            num_scalar_prefetch=1,
            grid=(STEPS,),
            in_specs=[
                pl.BlockSpec((GRP, BLK, D), near_map),
                pl.BlockSpec((GRP, BLK, D), far_map),
                pl.BlockSpec((TILE, DOCS), lambda s, b: (s, 0)),
                pl.BlockSpec((1, 1, DOCS), lambda s, b: (s, 0, 0)),
                pl.BlockSpec((1, DOCS), lambda s, b: (0, 0)),
                pl.BlockSpec((4, DOCS), lambda s, b: (0, 0)),
            ],
            out_specs=(
                pl.BlockSpec((TILE, DOCS), lambda s, b: (s, 0)),
                pl.BlockSpec((DOCS, D), lambda s, b: (0, 0)),
            ),
            scratch_shapes=[pltpu.VMEM((TILE, D), BF16), pltpu.VMEM((DOCS, D), F32)],
        ),
        compiler_params=pltpu.CompilerParams(
            dimension_semantics=("arbitrary",), vmem_limit_bytes=40 << 20
        ),
        cost_estimate=pl.CostEstimate(
            flops=2 * NB * LAB * DOCS * D, bytes_accessed=20 << 20, transcendentals=0
        ),
        name="second_pass",
    )(bases, near, far, exps, tops, log_total, positives)


def spread(chunks):
    return lax.all_to_all(chunks, "z", 0, 0)


def everywhere(block):
    return spread(jnp.broadcast_to(block[None], (8,) + block.shape))


def local(documents, label_weight, sample_ids, positive_cols, up_weight, down_weight):
    yh, yl = lax.axis_index("yh"), lax.axis_index("yl")
    x, core, z = lax.axis_index("x"), lax.axis_index("core"), lax.axis_index("z")
    plane_y = ("yh", "yl")
    units = down_weight.shape[0]

    up_rows = up_weight.T
    mine = jnp.where(core == 0, up_rows, down_weight)
    got = move(mine, "yl", 2, 1)
    got_other = move(got, "core", 2, 1)
    up_far = jnp.where(core == 0, got, got_other)
    down_far = jnp.where(core == 0, got_other, got)
    up_all = jnp.concatenate([jnp.where(yl == 0, up_rows, up_far), jnp.where(yl == 0, up_far, up_rows)], axis=0)
    down_all = jnp.concatenate(
        [jnp.where(yl == 0, down_weight, down_far), jnp.where(yl == 0, down_far, down_weight)], axis=0
    )

    log_expect = log_expected(sample_ids, label_weight.shape[0] * 256)
    piece_a = rounded(log_expect)
    piece_b = rounded(log_expect - piece_a)
    piece_c = log_expect - piece_a - piece_b
    pieces = jnp.stack([piece_a, piece_b, piece_c]).astype(BF16)
    pieces = jnp.pad(pieces, ((0, EXTRA - 3), (0, D - LAB)))
    block = jnp.concatenate([label_weight, pieces], axis=0)
    column = gather_ring(block, plane_y, 64)
    from_low = move(column, "x", 4, 1)
    from_high = move(column, "x", 4, -1)

    which = jnp.arange(NB, dtype=I32)
    rel = jnp.array(REL, I32)
    b_core = core ^ (which >> 4)
    b_x = (x + rel[(which >> 2) & 3]) % 4
    b_y = (yh * 2 + yl + rel[which & 3]) % 4
    bases = (((((b_y >> 1) * 4 + b_x) * 2 + b_core) * 16) + z * 2 + (b_y & 1)) * LAB

    docs = lax.dynamic_slice_in_dim(documents, yl * DOCS, DOCS, 0)
    pre_act = lax.dot_general(docs, up_all, NT, preferred_element_type=F32)
    hidden = jax.nn.gelu(pre_act, approximate=False).astype(BF16)
    partial_out = jnp.dot(hidden, down_all, preferred_element_type=F32).astype(BF16)
    parts = spread(partial_out.reshape(8, DOCS // 8, D))
    parts, from_low, from_high = lax.optimization_barrier((parts, from_low, from_high))
    own_docs = lax.dynamic_slice_in_dim(docs, z * (DOCS // 8), DOCS // 8, 0)
    own_emb = (own_docs.astype(F32) + total(parts)).astype(BF16)
    far_a = move(from_low[: 2 * BLK], "x", 4, 1)
    far_b = move(from_high[2 * BLK :], "x", 4, -1)
    near = jnp.concatenate([column, from_low, from_high, far_a, far_b], axis=0)
    far = move(near, "core", 2, 1)
    near = near.reshape(NB // 2, BLK, D)
    far = far.reshape(NB // 2, BLK, D)
    embedding = everywhere(own_emb).reshape(DOCS, D)

    exps, tops, stats = first_pass(near, far, embedding)
    all_stats = everywhere(stats)
    maxes, sums = all_stats[:, :4], all_stats[:, 4:]
    row_top = jnp.max(maxes, axis=0)
    row_total = jnp.sum(sums * jnp.exp(maxes - row_top[None]), axis=0)
    log_total = (row_top + jnp.log(row_total)).reshape(1, DOCS)
    positives = lax.dynamic_slice_in_dim(positive_cols, yl * DOCS, DOCS, 0).T
    grads, embed_part = second_pass(bases, near, far, exps, tops, log_total, positives)

    back = spread(embed_part.reshape(8, DOCS // 8, D))
    far_term = jnp.dot(grads[NB * LAB // 2 :], embedding, preferred_element_type=F32).astype(BF16)
    far_term = move(far_term, "core", 2, 1)
    back, grads, far_term = lax.optimization_barrier((back, grads, far_term))
    own_grad = total(back).astype(BF16)
    embed_grad = everywhere(own_grad).reshape(DOCS, D)

    side = NB * LAB // 2
    near_term = jnp.dot(grads[:side], embedding, preferred_element_type=F32).astype(BF16)
    chip = add(near_term, far_term).astype(BF16)
    col_sum = scatter_ring(chip.reshape(4, side // 4, D), "x", side // 8).astype(BF16)
    label_grad = scatter_ring(col_sum.reshape(4, LAB, D), plane_y, LAB // 2)

    act_grad = lax.dot_general(embed_grad, down_all, NT, preferred_element_type=F32)
    _, gelu_pull = jax.vjp(partial(jax.nn.gelu, approximate=False), pre_act)
    pre_grad = gelu_pull(act_grad)[0].astype(BF16)
    pieces = []
    for j in range(2):
        cols = slice(j * units, (j + 1) * units)
        up_term = lax.dot_general(docs, pre_grad[:, cols], TN, preferred_element_type=F32)
        down_term = lax.dot_general(embed_grad, hidden[:, cols], TN, preferred_element_type=F32)
        pieces.append(jnp.concatenate([up_term, down_term], axis=1).astype(BF16))
    rows = D // 16
    terms = jnp.stack(pieces).reshape(2, 8, 2, rows, 2 * units)
    keep = jnp.where(core == 0, terms[:, :, 0], terms[:, :, 1])
    give = jnp.where(core == 0, terms[:, :, 1], terms[:, :, 0])
    both = add(keep, move(give, "core", 2, 1)).astype(BF16)
    both = jnp.swapaxes(both, 0, 1).reshape(16, rows, 2 * units)
    mlp = total(lax.all_to_all(both, ("yh", "x", "yl"), 0, 0))
    return (label_grad, mlp[:, :units], mlp[:, units:].T)


def solution(mesh):
    cut = Mesh(np.asarray(mesh.devices).reshape(2, 4, 2, 8, 2), ("yh", "x", "core", "z", "yl"))
    wide, narrow = ("yh", "x", "core"), ("z", "yl")
    in_specs = (
        P(wide, None),
        P(wide + narrow, None),
        P(wide + narrow),
        P(wide, None),
        P(None, narrow),
        P(narrow, None),
    )
    out_specs = (P(wide + narrow, None), P(wide, narrow), P(narrow, wide))
    return jax.shard_map(local, mesh=cut, in_specs=in_specs, out_specs=out_specs, check_vma=False)
```

```python
from functools import partial

import jax
import jax.numpy as jnp
import numpy as np
from jax import lax
from jax.experimental import pallas as pl
from jax.experimental.pallas import tpu as pltpu
from jax.sharding import Mesh
from jax.sharding import PartitionSpec as P


CATALOG = 2812281
BF16, F32, I32 = jnp.bfloat16, jnp.float32, jnp.int32
D = 768
LAB = 128
EXTRA = 8
BLK = LAB + EXTRA
NB = 32
GRP = 4
TILE = GRP * LAB
STEPS = NB // GRP
DOCS = 512
REL = (0, -1, 1, 2)
NT = (((1,), (1,)), ((), ()))
TN = (((0,), (0,)), ((), ()))


def move(block, axes, size, distance):
    return lax.ppermute(block, axes, [(i, (i + distance) % size) for i in range(size)])


def add(a, b):
    return a.astype(F32) + b.astype(F32)


def total(parts):
    result = parts[0].astype(F32)
    for j in range(1, parts.shape[0]):
        result = result + parts[j].astype(F32)
    return result


def rounded(values):
    return lax.reduce_precision(values, 8, 7)


def log_expected(rank_ids, sampled):
    rank_float = rank_ids.astype(F32)
    return (
        jnp.log(F32(sampled))
        + jnp.log(jnp.log1p(1.0 / (rank_float + 1.0)))
        - jnp.log(jnp.log(F32(CATALOG) + 1.0))
    )


def fetch_labels(label_refs, rows, extras, sems):
    copies = []
    for g in range(STEPS):
        side, dx = g // 4, g % 4
        if dx < 3:
            sources = [(label_refs[side * 5 + dx], 0, GRP)]
        else:
            half = GRP // 2
            sources = [(label_refs[side * 5 + 3], 0, half), (label_refs[side * 5 + 4], half, half)]
        for n, (ref, at, size) in enumerate(sources):
            span = pl.ds(at, size)
            copies.append(
                (g, pltpu.make_async_copy(ref.at[:, pl.ds(0, LAB), :], rows.at[g, span], sems.at[g, 2 * n]))
            )
            if extras is not None:
                copies.append(
                    (
                        g,
                        pltpu.make_async_copy(
                            ref.at[:, pl.ds(LAB, EXTRA), pl.ds(0, LAB)],
                            extras.at[g, span],
                            sems.at[g, 2 * n + 1],
                        ),
                    )
                )
    return copies


def start_and_wait(copies):
    step = pl.program_id(0)

    @pl.when(step == 0)
    def _():
        for _, copy in copies:
            copy.start()

    for g in range(STEPS):

        @pl.when(step == g)
        def _():
            for at, copy in copies:
                if at == g:
                    copy.wait()


def first_kernel(*refs):
    label_refs = refs[:10]
    emb_ref, exp_ref, top_ref, stat_ref, rows, extras, sems, raw_a, raw_b, bias_a, bias_b, run_max, run_sum = refs[10:]
    step = pl.program_id(0)
    start_and_wait(fetch_labels(label_refs, rows, extras, sems))
    group = jnp.minimum(step, STEPS - 1)

    def body(raw_out, bias_out, raw_in, bias_in):
        lhs = rows[group].reshape(TILE, D)
        raw_out[...] = lax.dot_general(lhs, emb_ref[...], NT, preferred_element_type=F32)
        for j in range(GRP):
            pieces = extras[group, j].astype(F32)
            row = pieces[0:1] + pieces[1:2] + pieces[2:3]
            bias_out[j * LAB : (j + 1) * LAB, :] = jnp.broadcast_to(row, (LAB, LAB)).T
        for h in range(DOCS // LAB):
            cols = slice(h * LAB, (h + 1) * LAB)
            logits = raw_in[:, cols] - bias_in[...]
            old = run_max[:, cols]
            new = jnp.maximum(old, jnp.max(logits, axis=0, keepdims=True))
            exps = jnp.exp(logits - new)
            exp_ref[:, cols] = exps
            run_sum[:, cols] = run_sum[:, cols] * jnp.exp(old - new) + jnp.sum(exps, axis=0, keepdims=True)
            run_max[:, cols] = new

    @pl.when(lax.rem(step, 2) == 0)
    def _():
        body(raw_a, bias_a, raw_b, bias_b)

    @pl.when(lax.rem(step, 2) == 1)
    def _():
        body(raw_b, bias_b, raw_a, bias_a)

    @pl.when(step == 0)
    def _():
        run_max[...] = jnp.full_like(run_max, -jnp.inf)
        run_sum[...] = jnp.zeros_like(run_sum)

    top_ref[0] = run_max[...]

    @pl.when(step == STEPS)
    def _():
        for j in range(4):
            stat_ref[j : j + 1, :] = run_max[:, j * 128 : (j + 1) * 128]
            stat_ref[4 + j : 5 + j, :] = run_sum[:, j * 128 : (j + 1) * 128]


def second_kernel(base_ref, *refs):
    label_refs = refs[:10]
    exp_ref, top_ref, total_ref, pos_ref, grad_ref, out_ref, rows, sems, grad_a, grad_b, acc = refs[10:]
    step = pl.program_id(0)
    start_and_wait(fetch_labels(label_refs, rows, None, sems))
    group = jnp.minimum(step, STEPS - 1)
    before = jnp.maximum(step - 1, 0)

    def body(grad_out, grad_in):
        scale = jnp.exp(top_ref[0] - total_ref[...])
        pos = [pos_ref[k : k + 1, :] for k in range(4)]
        weights = []
        for k in range(4):
            same = [jnp.where(pos[k] == pos[n], F32(0.25), F32(0.0)) for n in range(4)]
            weights.append(same[0] + same[1] + same[2] + same[3])
        for j in range(GRP):
            span = slice(j * LAB, (j + 1) * LAB)
            base = base_ref[group * GRP + j]
            for h in range(DOCS // LAB):
                cols = slice(h * LAB, (h + 1) * LAB)
                ids = lax.broadcasted_iota(I32, (LAB, LAB), 0)
                hits = jnp.zeros((LAB, LAB), F32)
                for k in (3, 2, 1, 0):
                    hits = jnp.where(pos[k][:, cols] - base == ids, weights[k][:, cols], hits)
                grads = (exp_ref[span, cols] * scale[:, cols] - hits).astype(BF16)
                grad_ref[0, span, cols] = grads
                grad_out[span, cols] = grads
        acc[...] += lax.dot_general(
            grad_in[...], rows[before].reshape(TILE, D), TN, preferred_element_type=F32
        )

    @pl.when(lax.rem(step, 2) == 0)
    def _():
        body(grad_a, grad_b)

    @pl.when(lax.rem(step, 2) == 1)
    def _():
        body(grad_b, grad_a)

    @pl.when(step == 0)
    def _():
        acc[...] = jnp.zeros_like(acc)

    @pl.when(step == STEPS)
    def _():
        out_ref[...] = acc[...].astype(BF16)


def label_specs():
    return [pl.BlockSpec(memory_space=pl.ANY)] * 10


def behind(step, *_):
    return (jnp.maximum(step - 1, 0), 0)


def first_pass(labels, embedding):
    return pl.pallas_call(
        first_kernel,
        out_shape=(
            jax.ShapeDtypeStruct((NB * LAB, DOCS), F32),
            jax.ShapeDtypeStruct((STEPS, 1, DOCS), F32),
            jax.ShapeDtypeStruct((8, 128), F32),
        ),
        grid=(STEPS + 1,),
        in_specs=label_specs() + [pl.BlockSpec((DOCS, D), lambda s: (0, 0))],
        out_specs=(
            pl.BlockSpec((TILE, DOCS), behind),
            pl.BlockSpec((1, 1, DOCS), lambda s: (jnp.maximum(s - 1, 0), 0, 0)),
            pl.BlockSpec((8, 128), lambda s: (0, 0)),
        ),
        scratch_shapes=[
            pltpu.VMEM((STEPS, GRP, LAB, D), BF16),
            pltpu.VMEM((STEPS, GRP, EXTRA, LAB), BF16),
            pltpu.SemaphoreType.DMA((STEPS, 4)),
            pltpu.VMEM((TILE, DOCS), F32),
            pltpu.VMEM((TILE, DOCS), F32),
            pltpu.VMEM((TILE, LAB), F32),
            pltpu.VMEM((TILE, LAB), F32),
            pltpu.VMEM((1, DOCS), F32),
            pltpu.VMEM((1, DOCS), F32),
        ],
        compiler_params=pltpu.CompilerParams(
            dimension_semantics=("arbitrary",), vmem_limit_bytes=32 << 20
        ),
        cost_estimate=pl.CostEstimate(
            flops=2 * NB * LAB * DOCS * D, bytes_accessed=16 << 20, transcendentals=NB * LAB * DOCS
        ),
        name="first_pass",
    )(*labels, embedding)


def second_pass(bases, labels, exps, tops, log_total, positives):
    last = STEPS - 1
    return pl.pallas_call(
        second_kernel,
        out_shape=(
            jax.ShapeDtypeStruct((STEPS, TILE, DOCS), BF16),
            jax.ShapeDtypeStruct((DOCS, D), BF16),
        ),
        grid_spec=pltpu.PrefetchScalarGridSpec(
            num_scalar_prefetch=1,
            grid=(STEPS + 1,),
            in_specs=label_specs()
            + [
                pl.BlockSpec((TILE, DOCS), lambda s, b: (jnp.minimum(s, last), 0)),
                pl.BlockSpec((1, 1, DOCS), lambda s, b: (jnp.minimum(s, last), 0, 0)),
                pl.BlockSpec((1, DOCS), lambda s, b: (0, 0)),
                pl.BlockSpec((4, DOCS), lambda s, b: (0, 0)),
            ],
            out_specs=(
                pl.BlockSpec((1, TILE, DOCS), lambda s, b: (jnp.minimum(s, last), 0, 0)),
                pl.BlockSpec((DOCS, D), lambda s, b: (0, 0)),
            ),
            scratch_shapes=[
                pltpu.VMEM((STEPS, GRP, LAB, D), BF16),
                pltpu.SemaphoreType.DMA((STEPS, 4)),
                pltpu.VMEM((TILE, DOCS), BF16),
                pltpu.VMEM((TILE, DOCS), BF16),
                pltpu.VMEM((DOCS, D), F32),
            ],
        ),
        compiler_params=pltpu.CompilerParams(
            dimension_semantics=("arbitrary",), vmem_limit_bytes=32 << 20
        ),
        cost_estimate=pl.CostEstimate(
            flops=2 * NB * LAB * DOCS * D, bytes_accessed=20 << 20, transcendentals=0
        ),
        name="second_pass",
    )(bases, *labels, exps, tops, log_total, positives)


def spread(chunks):
    return lax.all_to_all(chunks, "z", 0, 0)


def everywhere(block):
    return spread(jnp.broadcast_to(block[None], (8,) + block.shape))


def step_of(documents, label_weight, sample_ids, positive_cols, up_weight, down_weight):
    yh, yl = lax.axis_index("yh"), lax.axis_index("yl")
    x, core, z = lax.axis_index("x"), lax.axis_index("core"), lax.axis_index("z")
    plane_y = ("yh", "yl")
    units = down_weight.shape[0]

    log_expect = log_expected(sample_ids, label_weight.shape[0] * 256)
    piece_a = rounded(log_expect)
    piece_b = rounded(log_expect - piece_a)
    piece_c = log_expect - piece_a - piece_b
    pieces = jnp.stack([piece_a, piece_b, piece_c]).astype(BF16)
    pieces = jnp.pad(pieces, ((0, EXTRA - 3), (0, D - LAB)))
    block = jnp.concatenate([label_weight, pieces], axis=0)
    y_low = move(block, plane_y, 4, 1)
    y_high = move(block, plane_y, 4, -1)
    y_far_a = move(y_low[:64], plane_y, 4, 1)
    y_far_b = move(y_high[64:], plane_y, 4, -1)
    column = jnp.concatenate([block, y_low, y_high, y_far_a, y_far_b], axis=0)
    x_low = move(column, "x", 4, 1)
    x_high = move(column, "x", 4, -1)
    c_column = move(column, "core", 2, 1)

    up_rows = up_weight.T
    mine = jnp.where(core == 0, up_rows, down_weight)
    got = move(mine, "yl", 2, 1)
    got_other = move(got, "core", 2, 1)
    up_far = jnp.where(core == 0, got, got_other)
    down_far = jnp.where(core == 0, got_other, got)
    up_all = jnp.concatenate([jnp.where(yl == 0, up_rows, up_far), jnp.where(yl == 0, up_far, up_rows)], axis=0)
    down_all = jnp.concatenate(
        [jnp.where(yl == 0, down_weight, down_far), jnp.where(yl == 0, down_far, down_weight)], axis=0
    )

    docs = lax.dynamic_slice_in_dim(documents, yl * DOCS, DOCS, 0)
    pre_act = lax.dot_general(docs, up_all, NT, preferred_element_type=F32)
    hidden = jax.nn.gelu(pre_act, approximate=False).astype(BF16)
    partial_out = jnp.dot(hidden, down_all, preferred_element_type=F32).astype(BF16)
    parts = spread(partial_out.reshape(8, DOCS // 8, D))
    parts, x_low, x_high = lax.optimization_barrier((parts, x_low, x_high))
    own_docs = lax.dynamic_slice_in_dim(docs, z * (DOCS // 8), DOCS // 8, 0)
    own_emb = (own_docs.astype(F32) + total(parts)).astype(BF16)
    x_far_a = move(x_low[: 2 * BLK], "x", 4, 1)
    x_far_b = move(x_high[2 * BLK :], "x", 4, -1)
    c_low = move(x_low, "core", 2, 1)
    c_high = move(x_high, "core", 2, 1)
    c_far_a = move(x_far_a, "core", 2, 1)
    c_far_b = move(x_far_b, "core", 2, 1)
    embedding = everywhere(own_emb).reshape(DOCS, D)
    near = [column, x_low, x_high, x_far_a, x_far_b]
    far = [c_column, c_low, c_high, c_far_a, c_far_b]
    labels = [part.reshape(-1, BLK, D) for part in near + far]

    which = jnp.arange(NB, dtype=I32)
    rel = jnp.array(REL, I32)
    b_core = core ^ (which >> 4)
    b_x = (x + rel[(which >> 2) & 3]) % 4
    b_y = (yh * 2 + yl + rel[which & 3]) % 4
    bases = (((((b_y >> 1) * 4 + b_x) * 2 + b_core) * 16) + z * 2 + (b_y & 1)) * LAB

    exps, tops, stats = first_pass(labels, embedding)
    all_stats = everywhere(stats)
    maxes, sums = all_stats[:, :4], all_stats[:, 4:]
    row_top = jnp.max(maxes, axis=0)
    row_total = jnp.sum(sums * jnp.exp(maxes - row_top[None]), axis=0)
    log_total = (row_top + jnp.log(row_total)).reshape(1, DOCS)
    positives = lax.dynamic_slice_in_dim(positive_cols, yl * DOCS, DOCS, 0).T
    grads, embed_part = second_pass(bases, labels, exps, tops, log_total, positives)

    back = spread(embed_part.reshape(8, DOCS // 8, D))
    own_grad = total(back).astype(BF16)
    embed_grad = everywhere(own_grad).reshape(DOCS, D)

    sums = [None] * 4
    for g in (3, 2, 1, 0):
        far_term = jnp.dot(grads[4 + g], embedding, preferred_element_type=F32).astype(BF16)
        far_term = move(far_term, "core", 2, 1)
        near_term = jnp.dot(grads[g], embedding, preferred_element_type=F32)
        sums[g] = (near_term + far_term.astype(F32)).astype(BF16)
    half = TILE // 2
    low_a = move(sums[3][:half], "x", 4, 1)
    high_b = move(sums[3][half:], "x", 4, -1)
    up_hi = move(sums[2][half:], "x", 4, 1)
    down_lo = move(sums[1][:half], "x", 4, -1)
    up_lo = add(sums[2][:half], low_a).astype(BF16)
    down_hi = add(sums[1][half:], high_b).astype(BF16)
    up_lo = move(up_lo, "x", 4, 1)
    down_hi = move(down_hi, "x", 4, -1)

    act_grad = lax.dot_general(embed_grad, down_all, NT, preferred_element_type=F32)
    _, gelu_pull = jax.vjp(partial(jax.nn.gelu, approximate=False), pre_act)
    pre_grad = gelu_pull(act_grad)[0].astype(BF16)
    pieces = []
    for j in range(2):
        cols = slice(j * units, (j + 1) * units)
        up_term = lax.dot_general(docs, pre_grad[:, cols], TN, preferred_element_type=F32)
        down_term = lax.dot_general(embed_grad, hidden[:, cols], TN, preferred_element_type=F32)
        pieces.append(jnp.concatenate([up_term, down_term], axis=1).astype(BF16))
    rows = D // 16
    terms = jnp.stack(pieces).reshape(2, 8, 2, rows, 2 * units)
    keep = jnp.where(core == 0, terms[:, :, 0], terms[:, :, 1])
    give = jnp.where(core == 0, terms[:, :, 1], terms[:, :, 0])
    give, up_lo, up_hi, down_lo, down_hi = lax.optimization_barrier((give, up_lo, up_hi, down_lo, down_hi))
    given = move(give, "core", 2, 1)
    both = add(keep, given).astype(BF16)
    both = jnp.swapaxes(both, 0, 1).reshape(16, rows, 2 * units)
    mlp = total(lax.all_to_all(both, ("yh", "x", "yl"), 0, 0))

    lo = (add(sums[0][:half], up_lo) + down_lo.astype(F32)).astype(BF16)
    hi = (add(sums[0][half:], up_hi) + down_hi.astype(F32)).astype(BF16)
    y_sums = [lo[:LAB], lo[LAB:], hi[:LAB], hi[LAB:]]
    half = LAB // 2
    low_a = move(y_sums[3][:half], plane_y, 4, 1)
    high_b = move(y_sums[3][half:], plane_y, 4, -1)
    up = jnp.concatenate([add(y_sums[2][:half], low_a), y_sums[2][half:].astype(F32)], axis=0).astype(BF16)
    down = jnp.concatenate([y_sums[1][:half].astype(F32), add(y_sums[1][half:], high_b)], axis=0).astype(BF16)
    up = move(up, plane_y, 4, 1)
    down = move(down, plane_y, 4, -1)
    label_grad = add(y_sums[0], up) + down.astype(F32)
    return (label_grad, mlp[:, :units], mlp[:, units:].T)


def solution(mesh):
    cut = Mesh(np.asarray(mesh.devices).reshape(2, 4, 2, 8, 2), ("yh", "x", "core", "z", "yl"))
    wide, narrow = ("yh", "x", "core"), ("z", "yl")
    in_specs = (
        P(wide, None),
        P(wide + narrow, None),
        P(wide + narrow),
        P(wide, None),
        P(None, narrow),
        P(narrow, None),
    )
    out_specs = (P(wide + narrow, None), P(wide, narrow), P(narrow, wide))
    return jax.shard_map(step_of, mesh=cut, in_specs=in_specs, out_specs=out_specs, check_vma=False)
```

```python
from functools import partial

import jax
import jax.numpy as jnp
import numpy as np
from jax import lax
from jax.experimental import pallas as pl
from jax.experimental.pallas import tpu as pltpu
from jax.sharding import Mesh
from jax.sharding import PartitionSpec as P


CATALOG = 2812281
BF16, F32, I32 = jnp.bfloat16, jnp.float32, jnp.int32
D = 768
LAB = 128
EXTRA = 8
BLK = LAB + EXTRA
NB = 32
GRP = 4
TILE = GRP * LAB
STEPS = NB // GRP
DOCS = 512
REL = (0, -1, 1, 2)
NT = (((1,), (1,)), ((), ()))
TN = (((0,), (0,)), ((), ()))


def move(block, axes, size, distance):
    return lax.ppermute(block, axes, [(i, (i + distance) % size) for i in range(size)])


def add(a, b):
    return a.astype(F32) + b.astype(F32)


def total(parts):
    result = parts[0].astype(F32)
    for j in range(1, parts.shape[0]):
        result = result + parts[j].astype(F32)
    return result


def rounded(values):
    return lax.reduce_precision(values, 8, 7)


def log_expected(rank_ids, sampled):
    rank_float = rank_ids.astype(F32)
    return (
        jnp.log(F32(sampled))
        + jnp.log(jnp.log1p(1.0 / (rank_float + 1.0)))
        - jnp.log(jnp.log(F32(CATALOG) + 1.0))
    )


def fetch_labels(label_refs, rows, extras, sems):
    copies = []
    for g in range(STEPS):
        side, dx = g // 4, g % 4
        if dx < 3:
            sources = [(label_refs[side * 5 + dx], 0, GRP)]
        else:
            half = GRP // 2
            sources = [(label_refs[side * 5 + 3], 0, half), (label_refs[side * 5 + 4], half, half)]
        for n, (ref, at, size) in enumerate(sources):
            span = pl.ds(at, size)
            copies.append(
                (g, pltpu.make_async_copy(ref.at[:, pl.ds(0, LAB), :], rows.at[g, span], sems.at[g, 2 * n]))
            )
            if extras is not None:
                copies.append(
                    (
                        g,
                        pltpu.make_async_copy(
                            ref.at[:, pl.ds(LAB, EXTRA), pl.ds(0, LAB)],
                            extras.at[g, span],
                            sems.at[g, 2 * n + 1],
                        ),
                    )
                )
    return copies


def start_and_wait(copies):
    step = pl.program_id(0)

    @pl.when(step == 0)
    def _():
        for _, copy in copies:
            copy.start()

    for g in range(STEPS):

        @pl.when(step == g)
        def _():
            for at, copy in copies:
                if at == g:
                    copy.wait()


def first_kernel(*refs):
    label_refs = refs[:10]
    (emb_hbm, exp_hbm, top_ref, stat_ref, rows, extras, sems, emb, emb_sem) = refs[10:19]
    (raw_a, raw_b, bias_a, bias_b, exp_a, exp_b, exp_sem, run_max, run_sum) = refs[19:]
    step = pl.program_id(0)
    fetch_emb = pltpu.make_async_copy(emb_hbm, emb, emb_sem)

    @pl.when(step == 0)
    def _():
        fetch_emb.start()

    start_and_wait(fetch_labels(label_refs, rows, extras, sems))

    @pl.when(step == 0)
    def _():
        fetch_emb.wait()

    group = jnp.minimum(step, STEPS - 1)

    def put(exp_out, slot, which):
        return pltpu.make_async_copy(exp_out, exp_hbm.at[which], exp_sem.at[slot])

    def body(slot, raw_out, bias_out, raw_in, bias_in, exp_out):
        @pl.when(step >= 3)
        def _():
            put(exp_out, slot, step - 3).wait()

        for j in range(GRP):
            pieces = extras[group, j].astype(F32)
            row = pieces[0:1] + pieces[1:2] + pieces[2:3]
            bias_out[j * LAB : (j + 1) * LAB, :] = jnp.broadcast_to(row, (LAB, LAB)).T
        lhs = rows[group].reshape(TILE, D)
        for half in range(2):
            wide = slice(half * 256, (half + 1) * 256)
            raw_out[:, wide] = lax.dot_general(lhs, emb[wide, :], NT, preferred_element_type=F32)
            for h in range(2):
                cols = slice(half * 256 + h * LAB, half * 256 + (h + 1) * LAB)
                logits = raw_in[:, cols] - bias_in[...]
                old = run_max[:, cols]
                new = jnp.maximum(old, jnp.max(logits, axis=0, keepdims=True))
                exps = jnp.exp(logits - new)
                exp_out[:, cols] = exps
                run_sum[:, cols] = run_sum[:, cols] * jnp.exp(old - new) + jnp.sum(exps, axis=0, keepdims=True)
                run_max[:, cols] = new

        @pl.when(step >= 1)
        def _():
            put(exp_out, slot, step - 1).start()

        @pl.when(step == STEPS)
        def _():
            put(exp_b if slot == 0 else exp_a, 1 - slot, step - 2).wait()
            put(exp_out, slot, step - 1).wait()

    @pl.when(lax.rem(step, 2) == 0)
    def _():
        body(0, raw_a, bias_a, raw_b, bias_b, exp_a)

    @pl.when(lax.rem(step, 2) == 1)
    def _():
        body(1, raw_b, bias_b, raw_a, bias_a, exp_b)

    @pl.when(step == 0)
    def _():
        run_max[...] = jnp.full_like(run_max, -jnp.inf)
        run_sum[...] = jnp.zeros_like(run_sum)

    top_ref[0] = run_max[...]

    @pl.when(step == STEPS)
    def _():
        for j in range(4):
            stat_ref[j : j + 1, :] = run_max[:, j * 128 : (j + 1) * 128]
            stat_ref[4 + j : 5 + j, :] = run_sum[:, j * 128 : (j + 1) * 128]


def hits_kernel(base_ref, pos_ref, hits_ref):
    step = pl.program_id(0)
    pos = [pos_ref[k : k + 1, :] for k in range(4)]
    weights = []
    for k in range(4):
        same = [jnp.where(pos[k] == pos[n], F32(0.25), F32(0.0)) for n in range(4)]
        weights.append(same[0] + same[1] + same[2] + same[3])
    for h in range(DOCS // LAB):
        cols = slice(h * LAB, (h + 1) * LAB)
        ids = lax.broadcasted_iota(I32, (LAB, LAB), 0)

        def block(j, carry):
            base = base_ref[step * GRP + j]
            hits = jnp.zeros((LAB, LAB), F32)
            for k in (3, 2, 1, 0):
                hits = jnp.where(pos[k][:, cols] - base == ids, weights[k][:, cols], hits)
            hits_ref[0, pl.ds(pl.multiple_of(j * LAB, LAB), LAB), cols] = hits.astype(BF16)
            return carry

        lax.fori_loop(0, GRP, block, 0)


def second_kernel(*refs):
    label_refs = refs[:10]
    exp_ref, top_ref, total_ref, hits_ref, grad_hbm, out_ref = refs[10:16]
    rows, sems, grad_a, grad_b, grad_sem, acc = refs[16:]
    step = pl.program_id(0)
    start_and_wait(fetch_labels(label_refs, rows, None, sems))
    before = jnp.maximum(step - 1, 0)

    def put(grad, slot, which):
        return pltpu.make_async_copy(grad, grad_hbm.at[which], grad_sem.at[slot])

    def body(slot, grad_out, grad_in):
        @pl.when(step >= 2)
        def _():
            put(grad_out, slot, step - 2).wait()

        scale = jnp.exp(top_ref[0] - total_ref[...])
        for j in range(GRP):
            span = slice(j * LAB, (j + 1) * LAB)
            grad_out[span, :] = (exp_ref[0, span, :] * scale - hits_ref[0, span, :].astype(F32)).astype(BF16)
        acc[...] += lax.dot_general(
            grad_in[...], rows[before].reshape(TILE, D), TN, preferred_element_type=F32
        )

        @pl.when(step < STEPS)
        def _():
            put(grad_out, slot, step).start()

        @pl.when(step == STEPS)
        def _():
            put(grad_in, 1 - slot, step - 1).wait()

    @pl.when(lax.rem(step, 2) == 0)
    def _():
        body(0, grad_a, grad_b)

    @pl.when(lax.rem(step, 2) == 1)
    def _():
        body(1, grad_b, grad_a)

    @pl.when(step == 0)
    def _():
        acc[...] = jnp.zeros_like(acc)

    @pl.when(step == STEPS)
    def _():
        out_ref[...] = acc[...].astype(BF16)


def label_specs():
    return [pl.BlockSpec(memory_space=pl.ANY)] * 10


def first_pass(labels, embedding):
    return pl.pallas_call(
        first_kernel,
        out_shape=(
            pltpu.HBM((STEPS, TILE, DOCS), F32),
            jax.ShapeDtypeStruct((STEPS, 1, DOCS), F32),
            jax.ShapeDtypeStruct((8, 128), F32),
        ),
        grid=(STEPS + 1,),
        in_specs=label_specs() + [pl.BlockSpec(memory_space=pl.ANY)],
        out_specs=(
            pl.BlockSpec(memory_space=pl.ANY),
            pl.BlockSpec((1, 1, DOCS), lambda s: (jnp.maximum(s - 1, 0), 0, 0)),
            pl.BlockSpec((8, 128), lambda s: (0, 0)),
        ),
        scratch_shapes=[
            pltpu.VMEM((STEPS, GRP, LAB, D), BF16),
            pltpu.VMEM((STEPS, GRP, EXTRA, LAB), BF16),
            pltpu.SemaphoreType.DMA((STEPS, 4)),
            pltpu.VMEM((DOCS, D), BF16),
            pltpu.SemaphoreType.DMA,
            pltpu.VMEM((TILE, DOCS), F32),
            pltpu.VMEM((TILE, DOCS), F32),
            pltpu.VMEM((TILE, LAB), F32),
            pltpu.VMEM((TILE, LAB), F32),
            pltpu.VMEM((TILE, DOCS), F32),
            pltpu.VMEM((TILE, DOCS), F32),
            pltpu.SemaphoreType.DMA((2,)),
            pltpu.VMEM((1, DOCS), F32),
            pltpu.VMEM((1, DOCS), F32),
        ],
        compiler_params=pltpu.CompilerParams(
            dimension_semantics=("arbitrary",), vmem_limit_bytes=32 << 20
        ),
        cost_estimate=pl.CostEstimate(
            flops=2 * NB * LAB * DOCS * D, bytes_accessed=16 << 20, transcendentals=NB * LAB * DOCS
        ),
        name="first_pass",
    )(*labels, embedding)


def positive_hits(bases, positives):
    return pl.pallas_call(
        hits_kernel,
        out_shape=pltpu.HBM((STEPS, TILE, DOCS), BF16),
        grid_spec=pltpu.PrefetchScalarGridSpec(
            num_scalar_prefetch=1,
            grid=(STEPS,),
            in_specs=[pl.BlockSpec((4, DOCS), lambda s, b: (0, 0))],
            out_specs=pl.BlockSpec((1, TILE, DOCS), lambda s, b: (s, 0, 0)),
        ),
        compiler_params=pltpu.CompilerParams(dimension_semantics=("arbitrary",)),
        cost_estimate=pl.CostEstimate(
            flops=16 * NB * LAB * DOCS, bytes_accessed=4 << 20, transcendentals=0
        ),
        name="positive_hits",
    )(bases, positives)


def second_pass(labels, exps, tops, log_total, hits):
    last = STEPS - 1
    return pl.pallas_call(
        second_kernel,
        out_shape=(
            pltpu.HBM((STEPS, TILE, DOCS), BF16),
            pltpu.HBM((DOCS, D), BF16),
        ),
        grid=(STEPS + 1,),
        in_specs=label_specs()
        + [
            pl.BlockSpec((1, TILE, DOCS), lambda s: (jnp.minimum(s, last), 0, 0)),
            pl.BlockSpec((1, 1, DOCS), lambda s: (jnp.minimum(s, last), 0, 0)),
            pl.BlockSpec((1, DOCS), lambda s: (0, 0)),
            pl.BlockSpec((1, TILE, DOCS), lambda s: (jnp.minimum(s, last), 0, 0)),
        ],
        out_specs=(
            pl.BlockSpec(memory_space=pl.ANY),
            pl.BlockSpec((DOCS, D), lambda s: (0, 0)),
        ),
        scratch_shapes=[
            pltpu.VMEM((STEPS, GRP, LAB, D), BF16),
            pltpu.SemaphoreType.DMA((STEPS, 4)),
            pltpu.VMEM((TILE, DOCS), BF16),
            pltpu.VMEM((TILE, DOCS), BF16),
            pltpu.SemaphoreType.DMA((2,)),
            pltpu.VMEM((DOCS, D), F32),
        ],
        compiler_params=pltpu.CompilerParams(
            dimension_semantics=("arbitrary",), vmem_limit_bytes=32 << 20
        ),
        cost_estimate=pl.CostEstimate(
            flops=2 * NB * LAB * DOCS * D, bytes_accessed=20 << 20, transcendentals=0
        ),
        name="second_pass",
    )(*labels, exps, tops, log_total, hits)


def spread(chunks):
    return lax.all_to_all(chunks, "z", 0, 0)


def everywhere(block):
    return spread(jnp.broadcast_to(block[None], (8,) + block.shape))


def step_of(documents, label_weight, sample_ids, positive_cols, up_weight, down_weight):
    yh, yl = lax.axis_index("yh"), lax.axis_index("yl")
    x, core, z = lax.axis_index("x"), lax.axis_index("core"), lax.axis_index("z")
    plane_y = ("yh", "yl")
    units = down_weight.shape[0]

    log_expect = log_expected(sample_ids, label_weight.shape[0] * 256)
    piece_a = rounded(log_expect)
    piece_b = rounded(log_expect - piece_a)
    piece_c = log_expect - piece_a - piece_b
    pieces = jnp.stack([piece_a, piece_b, piece_c]).astype(BF16)
    pieces = jnp.pad(pieces, ((0, EXTRA - 3), (0, D - LAB)))
    block = jnp.concatenate([label_weight, pieces], axis=0)
    y_low = move(block, plane_y, 4, 1)
    y_high = move(block, plane_y, 4, -1)
    y_far_a = move(y_low[:64], plane_y, 4, 1)
    y_far_b = move(y_high[64:], plane_y, 4, -1)
    column = jnp.concatenate([block, y_low, y_high, y_far_a, y_far_b], axis=0)
    x_low = move(column, "x", 4, 1)
    x_high = move(column, "x", 4, -1)
    c_column = move(column, "core", 2, 1)

    up_rows = up_weight.T
    mine = jnp.where(core == 0, up_rows, down_weight)
    got = move(mine, "yl", 2, 1)
    got_other = move(got, "core", 2, 1)
    up_far = jnp.where(core == 0, got, got_other)
    down_far = jnp.where(core == 0, got_other, got)
    up_all = jnp.concatenate([jnp.where(yl == 0, up_rows, up_far), jnp.where(yl == 0, up_far, up_rows)], axis=0)
    down_all = jnp.concatenate(
        [jnp.where(yl == 0, down_weight, down_far), jnp.where(yl == 0, down_far, down_weight)], axis=0
    )

    docs = lax.dynamic_slice_in_dim(documents, yl * DOCS, DOCS, 0)
    pre_act = lax.dot_general(docs, up_all, NT, preferred_element_type=F32)
    hidden = jax.nn.gelu(pre_act, approximate=False).astype(BF16)
    partial_out = jnp.dot(hidden, down_all, preferred_element_type=F32).astype(BF16)
    parts = spread(partial_out.reshape(8, DOCS // 8, D))
    parts, x_low, x_high = lax.optimization_barrier((parts, x_low, x_high))
    own_docs = lax.dynamic_slice_in_dim(docs, z * (DOCS // 8), DOCS // 8, 0)
    own_emb = (own_docs.astype(F32) + total(parts)).astype(BF16)
    x_far_a = move(x_low[: 2 * BLK], "x", 4, 1)
    x_far_b = move(x_high[2 * BLK :], "x", 4, -1)
    c_low = move(x_low, "core", 2, 1)
    c_high = move(x_high, "core", 2, 1)
    c_far_a = move(x_far_a, "core", 2, 1)
    c_far_b = move(x_far_b, "core", 2, 1)
    embedding = everywhere(own_emb).reshape(DOCS, D)
    near = [column, x_low, x_high, x_far_a, x_far_b]
    far = [c_column, c_low, c_high, c_far_a, c_far_b]
    labels = [part.reshape(-1, BLK, D) for part in near + far]

    which = jnp.arange(NB, dtype=I32)
    rel = jnp.array(REL, I32)
    b_core = core ^ (which >> 4)
    b_x = (x + rel[(which >> 2) & 3]) % 4
    b_y = (yh * 2 + yl + rel[which & 3]) % 4
    bases = (((((b_y >> 1) * 4 + b_x) * 2 + b_core) * 16) + z * 2 + (b_y & 1)) * LAB

    exps, tops, stats = first_pass(labels, embedding)
    all_stats = everywhere(stats)
    maxes, sums = all_stats[:, :4], all_stats[:, 4:]
    row_top = jnp.max(maxes, axis=0)
    row_total = jnp.sum(sums * jnp.exp(maxes - row_top[None]), axis=0)
    log_total = (row_top + jnp.log(row_total)).reshape(1, DOCS)
    positives = lax.dynamic_slice_in_dim(positive_cols, yl * DOCS, DOCS, 0).T
    hits = positive_hits(bases, positives)
    grads, embed_part = second_pass(labels, exps, tops, log_total, hits)

    back = spread(embed_part.reshape(8, DOCS // 8, D))
    own_grad = total(back).astype(BF16)
    embed_grad = everywhere(own_grad).reshape(DOCS, D)

    far_all = jnp.dot(grads[4:].reshape(-1, DOCS), embedding, preferred_element_type=F32).astype(BF16)
    far_all = move(far_all, "core", 2, 1)
    far_all = far_all.reshape(4, TILE, D)
    near_term = jnp.dot(grads[3], embedding, preferred_element_type=F32)
    last_sum = (near_term + far_all[3].astype(F32)).astype(BF16)
    near_term = jnp.dot(grads[:3].reshape(-1, DOCS), embedding, preferred_element_type=F32)
    rest = (near_term + far_all[:3].reshape(-1, D).astype(F32)).astype(BF16).reshape(3, TILE, D)
    sums = [rest[0], rest[1], rest[2], last_sum]
    half = TILE // 2
    low_a = move(sums[3][:half], "x", 4, 1)
    high_b = move(sums[3][half:], "x", 4, -1)
    up_hi = move(sums[2][half:], "x", 4, 1)
    down_lo = move(sums[1][:half], "x", 4, -1)
    up_lo = add(sums[2][:half], low_a).astype(BF16)
    down_hi = add(sums[1][half:], high_b).astype(BF16)
    up_lo = move(up_lo, "x", 4, 1)
    down_hi = move(down_hi, "x", 4, -1)

    act_grad = lax.dot_general(embed_grad, down_all, NT, preferred_element_type=F32)
    _, gelu_pull = jax.vjp(partial(jax.nn.gelu, approximate=False), pre_act)
    pre_grad = gelu_pull(act_grad)[0].astype(BF16)
    pieces = []
    for j in range(2):
        cols = slice(j * units, (j + 1) * units)
        up_term = lax.dot_general(docs, pre_grad[:, cols], TN, preferred_element_type=F32)
        down_term = lax.dot_general(embed_grad, hidden[:, cols], TN, preferred_element_type=F32)
        pieces.append(jnp.concatenate([up_term, down_term], axis=1).astype(BF16))
    rows = D // 16
    terms = jnp.stack(pieces).reshape(2, 8, 2, rows, 2 * units)
    keep = jnp.where(core == 0, terms[:, :, 0], terms[:, :, 1])
    give = jnp.where(core == 0, terms[:, :, 1], terms[:, :, 0])
    give, up_lo, up_hi, down_lo, down_hi = lax.optimization_barrier((give, up_lo, up_hi, down_lo, down_hi))
    given = move(give, "core", 2, 1)
    both = add(keep, given).astype(BF16)
    both = jnp.swapaxes(both, 0, 1).reshape(16, rows, 2 * units)
    mlp = total(lax.all_to_all(both, ("yh", "x", "yl"), 0, 0))

    lo = (add(sums[0][:half], up_lo) + down_lo.astype(F32)).astype(BF16)
    hi = (add(sums[0][half:], up_hi) + down_hi.astype(F32)).astype(BF16)
    y_sums = [lo[:LAB], lo[LAB:], hi[:LAB], hi[LAB:]]
    half = LAB // 2
    low_a = move(y_sums[3][:half], plane_y, 4, 1)
    high_b = move(y_sums[3][half:], plane_y, 4, -1)
    up = jnp.concatenate([add(y_sums[2][:half], low_a), y_sums[2][half:].astype(F32)], axis=0).astype(BF16)
    down = jnp.concatenate([y_sums[1][:half].astype(F32), add(y_sums[1][half:], high_b)], axis=0).astype(BF16)
    up = move(up, plane_y, 4, 1)
    down = move(down, plane_y, 4, -1)
    label_grad = add(y_sums[0], up) + down.astype(F32)
    return (label_grad, mlp[:, :units], mlp[:, units:].T)


def solution(mesh):
    cut = Mesh(np.asarray(mesh.devices).reshape(2, 4, 2, 8, 2), ("yh", "x", "core", "z", "yl"))
    wide, narrow = ("yh", "x", "core"), ("z", "yl")
    in_specs = (
        P(wide, None),
        P(wide + narrow, None),
        P(wide + narrow),
        P(wide, None),
        P(None, narrow),
        P(narrow, None),
    )
    out_specs = (P(wide + narrow, None), P(wide, narrow), P(narrow, wide))
    return jax.shard_map(step_of, mesh=cut, in_specs=in_specs, out_specs=out_specs, check_vma=False)
```

```python
from functools import partial

import jax
import jax.numpy as jnp
import numpy as np
from jax import lax
from jax.experimental import pallas as pl
from jax.experimental.pallas import tpu as pltpu
from jax.sharding import Mesh
from jax.sharding import PartitionSpec as P


CATALOG = 2812281
BF16, F32, I32 = jnp.bfloat16, jnp.float32, jnp.int32
D = 768
LAB = 128
EXTRA = 8
BLK = LAB + EXTRA
NB = 32
GRP = 4
TILE = GRP * LAB
STEPS = NB // GRP
DOCS = 512
REL = (0, -1, 1, 2)
NT = (((1,), (1,)), ((), ()))
TN = (((0,), (0,)), ((), ()))


def move(block, axes, size, distance):
    return lax.ppermute(block, axes, [(i, (i + distance) % size) for i in range(size)])


def add(a, b):
    return a.astype(F32) + b.astype(F32)


def total(parts):
    result = parts[0].astype(F32)
    for j in range(1, parts.shape[0]):
        result = result + parts[j].astype(F32)
    return result


def rounded(values):
    return lax.reduce_precision(values, 8, 7)


def log_expected(rank_ids, sampled):
    rank_float = rank_ids.astype(F32)
    return (
        jnp.log(F32(sampled))
        + jnp.log(jnp.log1p(1.0 / (rank_float + 1.0)))
        - jnp.log(jnp.log(F32(CATALOG) + 1.0))
    )


def fetch_labels(label_refs, rows, extras, sems):
    copies = []
    for g in range(STEPS):
        side, dx = g // 4, g % 4
        if dx < 3:
            sources = [(label_refs[side * 5 + dx], 0, GRP)]
        else:
            half = GRP // 2
            sources = [(label_refs[side * 5 + 3], 0, half), (label_refs[side * 5 + 4], half, half)]
        for n, (ref, at, size) in enumerate(sources):
            span = pl.ds(at, size)
            copies.append(
                (g, pltpu.make_async_copy(ref.at[:, pl.ds(0, LAB), :], rows.at[g, span], sems.at[g, 2 * n]))
            )
            if extras is not None:
                copies.append(
                    (
                        g,
                        pltpu.make_async_copy(
                            ref.at[:, pl.ds(LAB, EXTRA), pl.ds(0, LAB)],
                            extras.at[g, span],
                            sems.at[g, 2 * n + 1],
                        ),
                    )
                )
    return copies


def start_and_wait(copies):
    step = pl.program_id(0)

    @pl.when(step == 0)
    def _():
        for _, copy in copies:
            copy.start()

    for g in range(STEPS):

        @pl.when(step == g)
        def _():
            for at, copy in copies:
                if at == g:
                    copy.wait()


def first_kernel(*refs):
    label_refs = refs[:10]
    (emb_hbm, exp_hbm, top_ref, stat_ref, rows, extras, sems, emb, emb_sem) = refs[10:19]
    (raw_a, raw_b, bias_a, bias_b, exp_a, exp_b, exp_sem, run_max, run_sum) = refs[19:]
    step = pl.program_id(0)
    fetch_emb = pltpu.make_async_copy(emb_hbm, emb, emb_sem)

    @pl.when(step == 0)
    def _():
        fetch_emb.start()

    start_and_wait(fetch_labels(label_refs, rows, extras, sems))

    @pl.when(step == 0)
    def _():
        fetch_emb.wait()

    group = jnp.minimum(step, STEPS - 1)

    def put(exp_out, slot, which):
        return pltpu.make_async_copy(exp_out, exp_hbm.at[which], exp_sem.at[slot])

    def body(slot, raw_out, bias_out, raw_in, bias_in, exp_out):
        @pl.when(step >= 3)
        def _():
            put(exp_out, slot, step - 3).wait()

        for j in range(GRP):
            pieces = extras[group, j].astype(F32)
            row = pieces[0:1] + pieces[1:2] + pieces[2:3]
            bias_out[j * LAB : (j + 1) * LAB, :] = jnp.broadcast_to(row, (LAB, LAB)).T
        lhs = rows[group].reshape(TILE, D)
        for half in range(2):
            wide = slice(half * 256, (half + 1) * 256)
            raw_out[:, wide] = lax.dot_general(lhs, emb[wide, :], NT, preferred_element_type=F32)
            for h in range(2):
                cols = slice(half * 256 + h * LAB, half * 256 + (h + 1) * LAB)
                logits = raw_in[:, cols] - bias_in[...]
                old = run_max[:, cols]
                new = jnp.maximum(old, jnp.max(logits, axis=0, keepdims=True))
                exps = jnp.exp(logits - new)
                exp_out[:, cols] = exps
                run_sum[:, cols] = run_sum[:, cols] * jnp.exp(old - new) + jnp.sum(exps, axis=0, keepdims=True)
                run_max[:, cols] = new

        @pl.when(step >= 1)
        def _():
            put(exp_out, slot, step - 1).start()

        @pl.when(step == STEPS)
        def _():
            put(exp_b if slot == 0 else exp_a, 1 - slot, step - 2).wait()
            put(exp_out, slot, step - 1).wait()

    @pl.when(lax.rem(step, 2) == 0)
    def _():
        body(0, raw_a, bias_a, raw_b, bias_b, exp_a)

    @pl.when(lax.rem(step, 2) == 1)
    def _():
        body(1, raw_b, bias_b, raw_a, bias_a, exp_b)

    @pl.when(step == 0)
    def _():
        run_max[...] = jnp.full_like(run_max, -jnp.inf)
        run_sum[...] = jnp.zeros_like(run_sum)

    top_ref[0] = run_max[...]

    @pl.when(step == STEPS)
    def _():
        for j in range(4):
            stat_ref[j : j + 1, :] = run_max[:, j * 128 : (j + 1) * 128]
            stat_ref[4 + j : 5 + j, :] = run_sum[:, j * 128 : (j + 1) * 128]


def hits_kernel(base_ref, pos_ref, hits_ref):
    step = pl.program_id(0)
    pos = [pos_ref[k : k + 1, :] for k in range(4)]
    weights = []
    for k in range(4):
        same = [jnp.where(pos[k] == pos[n], F32(0.25), F32(0.0)) for n in range(4)]
        weights.append(same[0] + same[1] + same[2] + same[3])
    for h in range(DOCS // LAB):
        cols = slice(h * LAB, (h + 1) * LAB)
        ids = lax.broadcasted_iota(I32, (LAB, LAB), 0)

        def block(j, carry):
            base = base_ref[step * GRP + j]
            hits = jnp.zeros((LAB, LAB), F32)
            for k in (3, 2, 1, 0):
                hits = jnp.where(pos[k][:, cols] - base == ids, weights[k][:, cols], hits)
            hits_ref[0, pl.ds(pl.multiple_of(j * LAB, LAB), LAB), cols] = hits.astype(BF16)
            return carry

        lax.fori_loop(0, GRP, block, 0)


def second_kernel(*refs):
    label_refs = refs[:10]
    exp_ref, top_ref, total_ref, hits_ref, near_hbm, near_end, far_hbm, far_end, out_ref = refs[10:19]
    rows, sems, grad_a, grad_b, grad_sem, acc = refs[19:]
    side = STEPS // 2
    step = pl.program_id(0)
    start_and_wait(fetch_labels(label_refs, rows, None, sems))
    before = jnp.maximum(step - 1, 0)

    def put(grad, slot, home, which):
        return pltpu.make_async_copy(grad, home.at[which], grad_sem.at[slot])

    def body(slot, grad_out, grad_in):
        @pl.when(step >= 2)
        def _():
            put(grad_out, slot, near_hbm, 0).wait()

        scale = jnp.exp(top_ref[0] - total_ref[...])
        for j in range(GRP):
            span = slice(j * LAB, (j + 1) * LAB)
            grad_out[span, :] = (exp_ref[0, span, :] * scale - hits_ref[0, span, :].astype(F32)).astype(BF16)
        acc[...] += lax.dot_general(
            grad_in[...], rows[before].reshape(TILE, D), TN, preferred_element_type=F32
        )

        @pl.when(step < side - 1)
        def _():
            put(grad_out, slot, near_hbm, step).start()

        @pl.when((step >= side) & (step < STEPS - 1))
        def _():
            put(grad_out, slot, far_hbm, step - side).start()

        if slot == 1:

            @pl.when(step == side - 1)
            def _():
                put(grad_out, slot, near_end, 0).start()

            @pl.when(step == STEPS - 1)
            def _():
                put(grad_out, slot, far_end, 0).start()

        @pl.when(step == STEPS)
        def _():
            put(grad_in, 1 - slot, far_end, 0).wait()

    @pl.when(lax.rem(step, 2) == 0)
    def _():
        body(0, grad_a, grad_b)

    @pl.when(lax.rem(step, 2) == 1)
    def _():
        body(1, grad_b, grad_a)

    @pl.when(step == 0)
    def _():
        acc[...] = jnp.zeros_like(acc)

    @pl.when(step == STEPS)
    def _():
        out_ref[...] = acc[...].astype(BF16)


def in_hbm(array):
    return pltpu.with_memory_space_constraint(array, pltpu.HBM)


def label_specs():
    return [pl.BlockSpec(memory_space=pl.ANY)] * 10


def first_pass(labels, embedding):
    return pl.pallas_call(
        first_kernel,
        out_shape=(
            pltpu.HBM((STEPS, TILE, DOCS), F32),
            jax.ShapeDtypeStruct((STEPS, 1, DOCS), F32),
            jax.ShapeDtypeStruct((8, 128), F32),
        ),
        grid=(STEPS + 1,),
        in_specs=label_specs() + [pl.BlockSpec(memory_space=pl.ANY)],
        out_specs=(
            pl.BlockSpec(memory_space=pl.ANY),
            pl.BlockSpec((1, 1, DOCS), lambda s: (jnp.maximum(s - 1, 0), 0, 0)),
            pl.BlockSpec((8, 128), lambda s: (0, 0)),
        ),
        scratch_shapes=[
            pltpu.VMEM((STEPS, GRP, LAB, D), BF16),
            pltpu.VMEM((STEPS, GRP, EXTRA, LAB), BF16),
            pltpu.SemaphoreType.DMA((STEPS, 4)),
            pltpu.VMEM((DOCS, D), BF16),
            pltpu.SemaphoreType.DMA,
            pltpu.VMEM((TILE, DOCS), F32),
            pltpu.VMEM((TILE, DOCS), F32),
            pltpu.VMEM((TILE, LAB), F32),
            pltpu.VMEM((TILE, LAB), F32),
            pltpu.VMEM((TILE, DOCS), F32),
            pltpu.VMEM((TILE, DOCS), F32),
            pltpu.SemaphoreType.DMA((2,)),
            pltpu.VMEM((1, DOCS), F32),
            pltpu.VMEM((1, DOCS), F32),
        ],
        compiler_params=pltpu.CompilerParams(
            dimension_semantics=("arbitrary",), vmem_limit_bytes=32 << 20
        ),
        cost_estimate=pl.CostEstimate(
            flops=2 * NB * LAB * DOCS * D, bytes_accessed=16 << 20, transcendentals=NB * LAB * DOCS
        ),
        name="first_pass",
    )(*labels, embedding)


def positive_hits(bases, positives):
    return pl.pallas_call(
        hits_kernel,
        out_shape=pltpu.HBM((STEPS, TILE, DOCS), BF16),
        grid_spec=pltpu.PrefetchScalarGridSpec(
            num_scalar_prefetch=1,
            grid=(STEPS,),
            in_specs=[pl.BlockSpec((4, DOCS), lambda s, b: (0, 0))],
            out_specs=pl.BlockSpec((1, TILE, DOCS), lambda s, b: (s, 0, 0)),
        ),
        compiler_params=pltpu.CompilerParams(dimension_semantics=("arbitrary",)),
        cost_estimate=pl.CostEstimate(
            flops=16 * NB * LAB * DOCS, bytes_accessed=4 << 20, transcendentals=0
        ),
        name="positive_hits",
    )(bases, positives)


def second_pass(labels, exps, tops, log_total, hits):
    last = STEPS - 1
    return pl.pallas_call(
        second_kernel,
        out_shape=(
            pltpu.HBM((STEPS // 2 - 1, TILE, DOCS), BF16),
            pltpu.HBM((1, TILE, DOCS), BF16),
            pltpu.HBM((STEPS // 2 - 1, TILE, DOCS), BF16),
            pltpu.HBM((1, TILE, DOCS), BF16),
            pltpu.HBM((DOCS, D), BF16),
        ),
        grid=(STEPS + 1,),
        in_specs=label_specs()
        + [
            pl.BlockSpec((1, TILE, DOCS), lambda s: (jnp.minimum(s, last), 0, 0)),
            pl.BlockSpec((1, 1, DOCS), lambda s: (jnp.minimum(s, last), 0, 0)),
            pl.BlockSpec((1, DOCS), lambda s: (0, 0)),
            pl.BlockSpec((1, TILE, DOCS), lambda s: (jnp.minimum(s, last), 0, 0)),
        ],
        out_specs=(
            pl.BlockSpec(memory_space=pl.ANY),
            pl.BlockSpec(memory_space=pl.ANY),
            pl.BlockSpec(memory_space=pl.ANY),
            pl.BlockSpec(memory_space=pl.ANY),
            pl.BlockSpec((DOCS, D), lambda s: (0, 0)),
        ),
        scratch_shapes=[
            pltpu.VMEM((STEPS, GRP, LAB, D), BF16),
            pltpu.SemaphoreType.DMA((STEPS, 4)),
            pltpu.VMEM((TILE, DOCS), BF16),
            pltpu.VMEM((TILE, DOCS), BF16),
            pltpu.SemaphoreType.DMA((2,)),
            pltpu.VMEM((DOCS, D), F32),
        ],
        compiler_params=pltpu.CompilerParams(
            dimension_semantics=("arbitrary",), vmem_limit_bytes=32 << 20
        ),
        cost_estimate=pl.CostEstimate(
            flops=2 * NB * LAB * DOCS * D, bytes_accessed=20 << 20, transcendentals=0
        ),
        name="second_pass",
    )(*labels, in_hbm(exps), tops, log_total, in_hbm(hits))


def spread(chunks):
    return lax.all_to_all(chunks, "z", 0, 0)


def everywhere(block):
    return spread(jnp.broadcast_to(block[None], (8,) + block.shape))


def step_of(documents, label_weight, sample_ids, positive_cols, up_weight, down_weight):
    yh, yl = lax.axis_index("yh"), lax.axis_index("yl")
    x, core, z = lax.axis_index("x"), lax.axis_index("core"), lax.axis_index("z")
    plane_y = ("yh", "yl")
    units = down_weight.shape[0]

    log_expect = log_expected(sample_ids, label_weight.shape[0] * 256)
    piece_a = rounded(log_expect)
    piece_b = rounded(log_expect - piece_a)
    piece_c = log_expect - piece_a - piece_b
    pieces = jnp.stack([piece_a, piece_b, piece_c]).astype(BF16)
    pieces = jnp.pad(pieces, ((0, EXTRA - 3), (0, D - LAB)))
    block = jnp.concatenate([label_weight, pieces], axis=0)
    y_low = move(block, plane_y, 4, 1)
    y_high = move(block, plane_y, 4, -1)
    y_far_a = move(y_low[:64], plane_y, 4, 1)
    y_far_b = move(y_high[64:], plane_y, 4, -1)
    column = jnp.concatenate([block, y_low, y_high, y_far_a, y_far_b], axis=0)
    x_low = move(column, "x", 4, 1)
    x_high = move(column, "x", 4, -1)
    c_column = move(column, "core", 2, 1)

    up_rows = up_weight.T
    mine = jnp.where(core == 0, up_rows, down_weight)
    got = move(mine, "yl", 2, 1)
    got_other = move(got, "core", 2, 1)
    up_far = jnp.where(core == 0, got, got_other)
    down_far = jnp.where(core == 0, got_other, got)
    up_all = jnp.concatenate([jnp.where(yl == 0, up_rows, up_far), jnp.where(yl == 0, up_far, up_rows)], axis=0)
    down_all = jnp.concatenate(
        [jnp.where(yl == 0, down_weight, down_far), jnp.where(yl == 0, down_far, down_weight)], axis=0
    )

    docs = lax.dynamic_slice_in_dim(documents, yl * DOCS, DOCS, 0)
    pre_act = lax.dot_general(docs, up_all, NT, preferred_element_type=F32)
    hidden = jax.nn.gelu(pre_act, approximate=False).astype(BF16)
    partial_out = jnp.dot(hidden, down_all, preferred_element_type=F32).astype(BF16)
    parts = spread(partial_out.reshape(8, DOCS // 8, D))
    own_docs = lax.dynamic_slice_in_dim(docs, z * (DOCS // 8), DOCS // 8, 0)
    own_emb = (own_docs.astype(F32) + total(parts)).astype(BF16)
    x_far_a = move(x_low[: 2 * BLK], "x", 4, 1)
    x_far_b = move(x_high[2 * BLK :], "x", 4, -1)
    c_low = move(x_low, "core", 2, 1)
    c_high = move(x_high, "core", 2, 1)
    c_far_a = move(x_far_a, "core", 2, 1)
    c_far_b = move(x_far_b, "core", 2, 1)
    embedding = everywhere(own_emb).reshape(DOCS, D)
    near = [column, x_low, x_high, x_far_a, x_far_b]
    far = [c_column, c_low, c_high, c_far_a, c_far_b]
    labels = [in_hbm(part.reshape(-1, BLK, D)) for part in near + far]

    which = jnp.arange(NB, dtype=I32)
    rel = jnp.array(REL, I32)
    b_core = core ^ (which >> 4)
    b_x = (x + rel[(which >> 2) & 3]) % 4
    b_y = (yh * 2 + yl + rel[which & 3]) % 4
    bases = (((((b_y >> 1) * 4 + b_x) * 2 + b_core) * 16) + z * 2 + (b_y & 1)) * LAB

    exps, tops, stats = first_pass(labels, in_hbm(embedding))
    all_stats = everywhere(stats)
    maxes, sums = all_stats[:, :4], all_stats[:, 4:]
    row_top = jnp.max(maxes, axis=0)
    row_total = jnp.sum(sums * jnp.exp(maxes - row_top[None]), axis=0)
    log_total = (row_top + jnp.log(row_total)).reshape(1, DOCS)
    positives = lax.dynamic_slice_in_dim(positive_cols, yl * DOCS, DOCS, 0).T
    hits = positive_hits(bases, positives)
    near_grads, near_end, far_grads, far_end, embed_part = second_pass(labels, exps, tops, log_total, hits)

    back = spread(embed_part.reshape(8, DOCS // 8, D))
    own_grad = total(back).astype(BF16)
    embed_grad = everywhere(own_grad).reshape(DOCS, D)

    far_last = jnp.dot(far_end[0], embedding, preferred_element_type=F32).astype(BF16)
    far_last = move(far_last, "core", 2, 1)
    far_rest = jnp.dot(far_grads.reshape(-1, DOCS), embedding, preferred_element_type=F32).astype(BF16)
    far_rest = move(far_rest, "core", 2, 1)
    near_term = jnp.dot(near_end[0], embedding, preferred_element_type=F32)
    last_sum = (near_term + far_last.astype(F32)).astype(BF16)
    near_term = jnp.dot(near_grads.reshape(-1, DOCS), embedding, preferred_element_type=F32)
    rest = (near_term + far_rest.astype(F32)).astype(BF16).reshape(3, TILE, D)
    sums = [rest[0], rest[1], rest[2], last_sum]
    half = TILE // 2
    low_a = move(sums[3][:half], "x", 4, 1)
    high_b = move(sums[3][half:], "x", 4, -1)
    up_hi = move(sums[2][half:], "x", 4, 1)
    down_lo = move(sums[1][:half], "x", 4, -1)
    up_lo = add(sums[2][:half], low_a).astype(BF16)
    down_hi = add(sums[1][half:], high_b).astype(BF16)
    up_lo = move(up_lo, "x", 4, 1)
    down_hi = move(down_hi, "x", 4, -1)

    act_grad = lax.dot_general(embed_grad, down_all, NT, preferred_element_type=F32)
    _, gelu_pull = jax.vjp(partial(jax.nn.gelu, approximate=False), pre_act)
    pre_grad = gelu_pull(act_grad)[0].astype(BF16)
    pieces = []
    for j in range(2):
        cols = slice(j * units, (j + 1) * units)
        up_term = lax.dot_general(docs, pre_grad[:, cols], TN, preferred_element_type=F32)
        down_term = lax.dot_general(embed_grad, hidden[:, cols], TN, preferred_element_type=F32)
        pieces.append(jnp.concatenate([up_term, down_term], axis=1).astype(BF16))
    rows = D // 16
    terms = jnp.stack(pieces).reshape(2, 8, 2, rows, 2 * units)
    keep = jnp.where(core == 0, terms[:, :, 0], terms[:, :, 1])
    give = jnp.where(core == 0, terms[:, :, 1], terms[:, :, 0])
    given = move(give, "core", 2, 1)
    both = add(keep, given).astype(BF16)
    both = jnp.swapaxes(both, 0, 1).reshape(16, rows, 2 * units)
    mlp = total(lax.all_to_all(both, ("yh", "x", "yl"), 0, 0))

    half = TILE // 2
    lo = (add(sums[0][:half], up_lo) + down_lo.astype(F32)).astype(BF16)
    hi = (add(sums[0][half:], up_hi) + down_hi.astype(F32)).astype(BF16)
    y_sums = [lo[:LAB], lo[LAB:], hi[:LAB], hi[LAB:]]
    half = LAB // 2
    low_a = move(y_sums[3][:half], plane_y, 4, 1)
    high_b = move(y_sums[3][half:], plane_y, 4, -1)
    up = jnp.concatenate([add(y_sums[2][:half], low_a), y_sums[2][half:].astype(F32)], axis=0).astype(BF16)
    down = jnp.concatenate([y_sums[1][:half].astype(F32), add(y_sums[1][half:], high_b)], axis=0).astype(BF16)
    up = move(up, plane_y, 4, 1)
    down = move(down, plane_y, 4, -1)
    label_grad = add(y_sums[0], up) + down.astype(F32)
    return (label_grad, mlp[:, :units], mlp[:, units:].T)


def solution(mesh):
    cut = Mesh(np.asarray(mesh.devices).reshape(2, 4, 2, 8, 2), ("yh", "x", "core", "z", "yl"))
    wide, narrow = ("yh", "x", "core"), ("z", "yl")
    in_specs = (
        P(wide, None),
        P(wide + narrow, None),
        P(wide + narrow),
        P(wide, None),
        P(None, narrow),
        P(narrow, None),
    )
    out_specs = (P(wide + narrow, None), P(wide, narrow), P(narrow, wide))
    return jax.shard_map(step_of, mesh=cut, in_specs=in_specs, out_specs=out_specs, check_vma=False)
```

```python
from functools import partial

import jax
import jax.numpy as jnp
import numpy as np
from jax import lax
from jax.experimental import pallas as pl
from jax.experimental.pallas import tpu as pltpu
from jax.sharding import Mesh
from jax.sharding import PartitionSpec as P


CATALOG = 2812281
BF16, F32, I32 = jnp.bfloat16, jnp.float32, jnp.int32
D = 768
LAB = 128
EXTRA = 8
BLK = LAB + EXTRA
NB = 32
GRP = 4
TILE = GRP * LAB
STEPS = NB // GRP
DOCS = 512
DOWN = 384
ROWS = D // 16
REL = (0, -1, 1, 2)
NT = (((1,), (1,)), ((), ()))
TN = (((0,), (0,)), ((), ()))


def move(block, axes, size, distance):
    return lax.ppermute(block, axes, [(i, (i + distance) % size) for i in range(size)])


def add(a, b):
    return a.astype(F32) + b.astype(F32)


def total(parts):
    result = parts[0].astype(F32)
    for j in range(1, parts.shape[0]):
        result = result + parts[j].astype(F32)
    return result


def rounded(values):
    return lax.reduce_precision(values, 8, 7)


def log_expected(rank_ids, sampled):
    rank_float = rank_ids.astype(F32)
    return (
        jnp.log(F32(sampled))
        + jnp.log(jnp.log1p(1.0 / (rank_float + 1.0)))
        - jnp.log(jnp.log(F32(CATALOG) + 1.0))
    )


def fetch_labels(label_refs, rows, extras, sems):
    copies = []
    for g in range(STEPS):
        side, dx = g // 4, g % 4
        if dx < 3:
            sources = [(label_refs[side * 5 + dx], 0, GRP)]
        else:
            half = GRP // 2
            sources = [(label_refs[side * 5 + 3], 0, half), (label_refs[side * 5 + 4], half, half)]
        for n, (ref, at, size) in enumerate(sources):
            span = pl.ds(at, size)
            copies.append(
                (g, pltpu.make_async_copy(ref.at[:, pl.ds(0, LAB), :], rows.at[g, span], sems.at[g, 2 * n]))
            )
            if extras is not None:
                copies.append(
                    (
                        g,
                        pltpu.make_async_copy(
                            ref.at[:, pl.ds(LAB, EXTRA), pl.ds(0, LAB)],
                            extras.at[g, span],
                            sems.at[g, 2 * n + 1],
                        ),
                    )
                )
    return copies


def start_and_wait(copies):
    step = pl.program_id(0)

    @pl.when(step == 0)
    def _():
        for _, copy in copies:
            copy.start()

    for g in range(STEPS):

        @pl.when(step == g)
        def _():
            for at, copy in copies:
                if at == g:
                    copy.wait()


def first_kernel(*refs):
    label_refs = refs[:10]
    (emb_hbm, exp_hbm, top_ref, stat_ref, rows, extras, sems, emb, emb_sem) = refs[10:19]
    (raw_a, raw_b, bias_a, bias_b, exp_a, exp_b, exp_sem, run_max, run_sum) = refs[19:]
    step = pl.program_id(0)
    fetch_emb = pltpu.make_async_copy(emb_hbm, emb, emb_sem)

    @pl.when(step == 0)
    def _():
        fetch_emb.start()

    start_and_wait(fetch_labels(label_refs, rows, extras, sems))

    @pl.when(step == 0)
    def _():
        fetch_emb.wait()

    group = jnp.minimum(step, STEPS - 1)

    def put(exp_out, slot, which):
        return pltpu.make_async_copy(exp_out, exp_hbm.at[which], exp_sem.at[slot])

    def body(slot, raw_out, bias_out, raw_in, bias_in, exp_out):
        @pl.when(step >= 3)
        def _():
            put(exp_out, slot, step - 3).wait()

        for j in range(GRP):
            pieces = extras[group, j].astype(F32)
            row = pieces[0:1] + pieces[1:2] + pieces[2:3]
            bias_out[j * LAB : (j + 1) * LAB, :] = jnp.broadcast_to(row, (LAB, LAB)).T
        lhs = rows[group].reshape(TILE, D)
        for half in range(2):
            wide = slice(half * 256, (half + 1) * 256)
            raw_out[:, wide] = lax.dot_general(lhs, emb[wide, :], NT, preferred_element_type=F32)
            for h in range(2):
                cols = slice(half * 256 + h * LAB, half * 256 + (h + 1) * LAB)
                logits = raw_in[:, cols] - bias_in[...]
                old = run_max[:, cols]
                new = jnp.maximum(old, jnp.max(logits, axis=0, keepdims=True))
                exps = jnp.exp(logits - new)
                exp_out[:, cols] = exps
                run_sum[:, cols] = run_sum[:, cols] * jnp.exp(old - new) + jnp.sum(exps, axis=0, keepdims=True)
                run_max[:, cols] = new

        @pl.when(step >= 1)
        def _():
            put(exp_out, slot, step - 1).start()

        @pl.when(step == STEPS)
        def _():
            put(exp_b if slot == 0 else exp_a, 1 - slot, step - 2).wait()
            put(exp_out, slot, step - 1).wait()

    @pl.when(lax.rem(step, 2) == 0)
    def _():
        body(0, raw_a, bias_a, raw_b, bias_b, exp_a)

    @pl.when(lax.rem(step, 2) == 1)
    def _():
        body(1, raw_b, bias_b, raw_a, bias_a, exp_b)

    @pl.when(step == 0)
    def _():
        run_max[...] = jnp.full_like(run_max, -jnp.inf)
        run_sum[...] = jnp.zeros_like(run_sum)

    top_ref[0] = run_max[...]

    @pl.when(step == STEPS)
    def _():
        for j in range(4):
            stat_ref[j : j + 1, :] = run_max[:, j * 128 : (j + 1) * 128]
            stat_ref[4 + j : 5 + j, :] = run_sum[:, j * 128 : (j + 1) * 128]


def hits_kernel(base_ref, pos_ref, docs_ref, hits_ref, turned_ref):
    step = pl.program_id(0)

    @pl.when(step == 0)
    def _():
        turned_ref[...] = docs_ref[...].T

    pos = [pos_ref[k : k + 1, :] for k in range(4)]
    weights = []
    for k in range(4):
        same = [jnp.where(pos[k] == pos[n], F32(0.25), F32(0.0)) for n in range(4)]
        weights.append(same[0] + same[1] + same[2] + same[3])
    for h in range(DOCS // LAB):
        cols = slice(h * LAB, (h + 1) * LAB)
        ids = lax.broadcasted_iota(I32, (LAB, LAB), 0)

        def block(j, carry):
            base = base_ref[step * GRP + j]
            hits = jnp.zeros((LAB, LAB), F32)
            for k in (3, 2, 1, 0):
                hits = jnp.where(pos[k][:, cols] - base == ids, weights[k][:, cols], hits)
            hits_ref[0, pl.ds(pl.multiple_of(j * LAB, LAB), LAB), cols] = hits.astype(BF16)
            return carry

        lax.fori_loop(0, GRP, block, 0)


def second_kernel(*refs):
    label_refs = refs[:10]
    exp_ref, top_ref, total_ref, hits_ref, near_hbm, near_end, far_hbm, far_end, out_ref = refs[10:19]
    rows, sems, grad_a, grad_b, grad_sem, acc = refs[19:]
    side = STEPS // 2
    step = pl.program_id(0)
    start_and_wait(fetch_labels(label_refs, rows, None, sems))
    before = jnp.maximum(step - 1, 0)

    def put(grad, slot, home, which):
        return pltpu.make_async_copy(grad, home.at[which], grad_sem.at[slot])

    def body(slot, grad_out, grad_in):
        @pl.when(step >= 2)
        def _():
            put(grad_out, slot, near_hbm, 0).wait()

        scale = jnp.exp(top_ref[0] - total_ref[...])
        for j in range(GRP):
            span = slice(j * LAB, (j + 1) * LAB)
            grad_out[span, :] = (exp_ref[0, span, :] * scale - hits_ref[0, span, :].astype(F32)).astype(BF16)
        acc[...] += lax.dot_general(
            grad_in[...], rows[before].reshape(TILE, D), TN, preferred_element_type=F32
        )

        @pl.when(step < side - 1)
        def _():
            put(grad_out, slot, near_hbm, step).start()

        @pl.when((step >= side) & (step < STEPS - 1))
        def _():
            put(grad_out, slot, far_hbm, step - side).start()

        if slot == 1:

            @pl.when(step == side - 1)
            def _():
                put(grad_out, slot, near_end, 0).start()

            @pl.when(step == STEPS - 1)
            def _():
                put(grad_out, slot, far_end, 0).start()

        @pl.when(step == STEPS)
        def _():
            put(grad_in, 1 - slot, far_end, 0).wait()

    @pl.when(lax.rem(step, 2) == 0)
    def _():
        body(0, grad_a, grad_b)

    @pl.when(lax.rem(step, 2) == 1)
    def _():
        body(1, grad_b, grad_a)

    @pl.when(step == 0)
    def _():
        acc[...] = jnp.zeros_like(acc)

    @pl.when(step == STEPS)
    def _():
        out_ref[...] = acc[...].astype(BF16)


def in_hbm(array):
    return pltpu.with_memory_space_constraint(array, pltpu.HBM)


def label_specs():
    return [pl.BlockSpec(memory_space=pl.ANY)] * 10


def first_pass(labels, embedding):
    return pl.pallas_call(
        first_kernel,
        out_shape=(
            jax.ShapeDtypeStruct((STEPS, TILE, DOCS), F32),
            jax.ShapeDtypeStruct((STEPS, 1, DOCS), F32),
            jax.ShapeDtypeStruct((8, 128), F32),
        ),
        grid=(STEPS + 1,),
        in_specs=label_specs() + [pl.BlockSpec(memory_space=pl.ANY)],
        out_specs=(
            pl.BlockSpec(memory_space=pl.ANY),
            pl.BlockSpec((1, 1, DOCS), lambda s: (jnp.maximum(s - 1, 0), 0, 0)),
            pl.BlockSpec((8, 128), lambda s: (0, 0)),
        ),
        scratch_shapes=[
            pltpu.VMEM((STEPS, GRP, LAB, D), BF16),
            pltpu.VMEM((STEPS, GRP, EXTRA, LAB), BF16),
            pltpu.SemaphoreType.DMA((STEPS, 4)),
            pltpu.VMEM((DOCS, D), BF16),
            pltpu.SemaphoreType.DMA,
            pltpu.VMEM((TILE, DOCS), F32),
            pltpu.VMEM((TILE, DOCS), F32),
            pltpu.VMEM((TILE, LAB), F32),
            pltpu.VMEM((TILE, LAB), F32),
            pltpu.VMEM((TILE, DOCS), F32),
            pltpu.VMEM((TILE, DOCS), F32),
            pltpu.SemaphoreType.DMA((2,)),
            pltpu.VMEM((1, DOCS), F32),
            pltpu.VMEM((1, DOCS), F32),
        ],
        compiler_params=pltpu.CompilerParams(
            dimension_semantics=("arbitrary",), vmem_limit_bytes=18 << 20
        ),
        cost_estimate=pl.CostEstimate(
            flops=2 * NB * LAB * DOCS * D, bytes_accessed=16 << 20, transcendentals=NB * LAB * DOCS
        ),
        name="first_pass",
    )(*labels, embedding)


def positive_hits(bases, positives, documents):
    return pl.pallas_call(
        hits_kernel,
        out_shape=(
            jax.ShapeDtypeStruct((STEPS, TILE, DOCS), BF16),
            jax.ShapeDtypeStruct((D, DOCS), BF16),
        ),
        grid_spec=pltpu.PrefetchScalarGridSpec(
            num_scalar_prefetch=1,
            grid=(STEPS,),
            in_specs=[
                pl.BlockSpec((4, DOCS), lambda s, b: (0, 0)),
                pl.BlockSpec((DOCS, D), lambda s, b: (b[NB], 0)),
            ],
            out_specs=(
                pl.BlockSpec((1, TILE, DOCS), lambda s, b: (s, 0, 0)),
                pl.BlockSpec((D, DOCS), lambda s, b: (0, 0)),
            ),
        ),
        compiler_params=pltpu.CompilerParams(dimension_semantics=("arbitrary",)),
        cost_estimate=pl.CostEstimate(
            flops=16 * NB * LAB * DOCS, bytes_accessed=4 << 20, transcendentals=0
        ),
        name="positive_hits",
    )(bases, positives, documents)


def mlp_kernel(core_ref, grad_ref, down_ref, slope_ref, hidden_ref, turned_ref, keep_ref, give_ref, both):
    units = DOWN // 2
    act_grad = lax.dot_general(grad_ref[...], down_ref[...], NT, preferred_element_type=F32)
    pre_grad = (act_grad * slope_ref[...]).astype(BF16)
    down_term = lax.dot_general(grad_ref[...], hidden_ref[...], TN, preferred_element_type=F32)
    up_term = jnp.dot(turned_ref[...], pre_grad, preferred_element_type=F32)
    for j in range(2):
        cols = slice(j * units, (j + 1) * units)
        both[j] = jnp.concatenate([up_term[:, cols], down_term[:, cols]], axis=1).astype(BF16)
    core = core_ref[0]
    for q in range(8):
        for j in range(2):
            mine = pl.multiple_of((2 * q + core) * ROWS, ROWS)
            other = pl.multiple_of((2 * q + 1 - core) * ROWS, ROWS)
            keep_ref[2 * q + j] = both[j, pl.ds(mine, ROWS), :]
            give_ref[2 * q + j] = both[j, pl.ds(other, ROWS), :]


def mlp_back(core, embed_grad, down_all, slope, hidden, turned):
    shape = jax.ShapeDtypeStruct((16, ROWS, DOWN), BF16)
    vmem = pl.BlockSpec(memory_space=pltpu.VMEM)
    return pl.pallas_call(
        mlp_kernel,
        out_shape=(shape, shape),
        in_specs=[pl.BlockSpec(memory_space=pltpu.SMEM)] + [vmem] * 5,
        out_specs=(vmem, vmem),
        scratch_shapes=[pltpu.VMEM((2, D, DOWN), BF16)],
        compiler_params=pltpu.CompilerParams(vmem_limit_bytes=24 << 20),
        cost_estimate=pl.CostEstimate(
            flops=6 * DOCS * D * DOWN, bytes_accessed=6 << 20, transcendentals=0
        ),
        name="mlp_back",
    )(core, embed_grad, down_all, slope, hidden, turned)


def second_pass(labels, exps, tops, log_total, hits):
    last = STEPS - 1
    return pl.pallas_call(
        second_kernel,
        out_shape=(
            pltpu.HBM((STEPS // 2 - 1, TILE, DOCS), BF16),
            pltpu.HBM((1, TILE, DOCS), BF16),
            pltpu.HBM((STEPS // 2 - 1, TILE, DOCS), BF16),
            pltpu.HBM((1, TILE, DOCS), BF16),
            pltpu.HBM((DOCS, D), BF16),
        ),
        grid=(STEPS + 1,),
        in_specs=label_specs()
        + [
            pl.BlockSpec((1, TILE, DOCS), lambda s: (jnp.minimum(s, last), 0, 0)),
            pl.BlockSpec((1, 1, DOCS), lambda s: (jnp.minimum(s, last), 0, 0)),
            pl.BlockSpec((1, DOCS), lambda s: (0, 0)),
            pl.BlockSpec((1, TILE, DOCS), lambda s: (jnp.minimum(s, last), 0, 0)),
        ],
        out_specs=(
            pl.BlockSpec(memory_space=pl.ANY),
            pl.BlockSpec(memory_space=pl.ANY),
            pl.BlockSpec(memory_space=pl.ANY),
            pl.BlockSpec(memory_space=pl.ANY),
            pl.BlockSpec((DOCS, D), lambda s: (0, 0)),
        ),
        scratch_shapes=[
            pltpu.VMEM((STEPS, GRP, LAB, D), BF16),
            pltpu.SemaphoreType.DMA((STEPS, 4)),
            pltpu.VMEM((TILE, DOCS), BF16),
            pltpu.VMEM((TILE, DOCS), BF16),
            pltpu.SemaphoreType.DMA((2,)),
            pltpu.VMEM((DOCS, D), F32),
        ],
        compiler_params=pltpu.CompilerParams(
            dimension_semantics=("arbitrary",), vmem_limit_bytes=18 << 20
        ),
        cost_estimate=pl.CostEstimate(
            flops=2 * NB * LAB * DOCS * D, bytes_accessed=20 << 20, transcendentals=0
        ),
        name="second_pass",
    )(*labels, exps, tops, log_total, hits)


def spread(chunks):
    return lax.all_to_all(chunks, "z", 0, 0)


def everywhere(block):
    return spread(jnp.broadcast_to(block[None], (8,) + block.shape))


def step_of(documents, label_weight, sample_ids, positive_cols, up_weight, down_weight):
    yh, yl = lax.axis_index("yh"), lax.axis_index("yl")
    x, core, z = lax.axis_index("x"), lax.axis_index("core"), lax.axis_index("z")
    plane_y = ("yh", "yl")
    units = down_weight.shape[0]

    log_expect = log_expected(sample_ids, label_weight.shape[0] * 256)
    piece_a = rounded(log_expect)
    piece_b = rounded(log_expect - piece_a)
    piece_c = log_expect - piece_a - piece_b
    pieces = jnp.stack([piece_a, piece_b, piece_c]).astype(BF16)
    pieces = jnp.pad(pieces, ((0, EXTRA - 3), (0, D - LAB)))
    block = jnp.concatenate([label_weight, pieces], axis=0)
    y_low = move(block, plane_y, 4, 1)
    y_high = move(block, plane_y, 4, -1)
    y_far_a = move(y_low[:64], plane_y, 4, 1)
    y_far_b = move(y_high[64:], plane_y, 4, -1)
    column = jnp.concatenate([block, y_low, y_high, y_far_a, y_far_b], axis=0)
    x_low = move(column, "x", 4, 1)
    x_high = move(column, "x", 4, -1)
    c_column = move(column, "core", 2, 1)

    up_rows = up_weight.T
    mine = jnp.where(core == 0, up_rows, down_weight)
    got = move(mine, "yl", 2, 1)
    got_other = move(got, "core", 2, 1)
    up_far = jnp.where(core == 0, got, got_other)
    down_far = jnp.where(core == 0, got_other, got)
    up_all = jnp.concatenate([jnp.where(yl == 0, up_rows, up_far), jnp.where(yl == 0, up_far, up_rows)], axis=0)
    down_all = jnp.concatenate(
        [jnp.where(yl == 0, down_weight, down_far), jnp.where(yl == 0, down_far, down_weight)], axis=0
    )

    docs = lax.dynamic_slice_in_dim(documents, yl * DOCS, DOCS, 0)
    pre_act = lax.dot_general(docs, up_all, NT, preferred_element_type=F32)
    hidden, gelu_pull = jax.vjp(partial(jax.nn.gelu, approximate=False), pre_act)
    hidden = hidden.astype(BF16)
    slope = gelu_pull(jnp.ones_like(pre_act))[0]
    partial_out = jnp.dot(hidden, down_all, preferred_element_type=F32).astype(BF16)
    parts = spread(partial_out.reshape(8, DOCS // 8, D))
    own_docs = lax.dynamic_slice_in_dim(docs, z * (DOCS // 8), DOCS // 8, 0)
    own_emb = (own_docs.astype(F32) + total(parts)).astype(BF16)
    x_far_a = move(x_low[: 2 * BLK], "x", 4, 1)
    x_far_b = move(x_high[2 * BLK :], "x", 4, -1)
    c_low = move(x_low, "core", 2, 1)
    c_high = move(x_high, "core", 2, 1)
    c_far_a = move(x_far_a, "core", 2, 1)
    c_far_b = move(x_far_b, "core", 2, 1)
    embedding = everywhere(own_emb).reshape(DOCS, D)
    near = [column, x_low, x_high, x_far_a, x_far_b]
    far = [c_column, c_low, c_high, c_far_a, c_far_b]
    labels = [in_hbm(part.reshape(-1, BLK, D)) for part in near + far]

    which = jnp.arange(NB, dtype=I32)
    rel = jnp.array(REL, I32)
    b_core = core ^ (which >> 4)
    b_x = (x + rel[(which >> 2) & 3]) % 4
    b_y = (yh * 2 + yl + rel[which & 3]) % 4
    bases = (((((b_y >> 1) * 4 + b_x) * 2 + b_core) * 16) + z * 2 + (b_y & 1)) * LAB

    exps, tops, stats = first_pass(labels, in_hbm(embedding))
    all_stats = everywhere(stats)
    maxes, sums = all_stats[:, :4], all_stats[:, 4:]
    row_top = jnp.max(maxes, axis=0)
    row_total = jnp.sum(sums * jnp.exp(maxes - row_top[None]), axis=0)
    log_total = (row_top + jnp.log(row_total)).reshape(1, DOCS)
    positives = lax.dynamic_slice_in_dim(positive_cols, yl * DOCS, DOCS, 0).T
    scalars = jnp.concatenate([bases, yl.reshape(1).astype(I32)])
    hits, turned = positive_hits(scalars, positives, documents)
    near_grads, near_end, far_grads, far_end, embed_part = second_pass(labels, exps, tops, log_total, hits)

    back = spread(embed_part.reshape(8, DOCS // 8, D))
    own_grad = total(back).astype(BF16)
    embed_grad = everywhere(own_grad).reshape(DOCS, D)

    far_last = jnp.dot(far_end[0], embedding, preferred_element_type=F32).astype(BF16)
    far_last = move(far_last, "core", 2, 1)
    far_rest = jnp.dot(far_grads.reshape(-1, DOCS), embedding, preferred_element_type=F32).astype(BF16)
    far_rest = move(far_rest, "core", 2, 1)
    near_term = jnp.dot(near_end[0], embedding, preferred_element_type=F32)
    last_sum = (near_term + far_last.astype(F32)).astype(BF16)
    near_term = jnp.dot(near_grads.reshape(-1, DOCS), embedding, preferred_element_type=F32)
    rest = (near_term + far_rest.astype(F32)).astype(BF16).reshape(3, TILE, D)
    sums = [rest[0], rest[1], rest[2], last_sum]
    half = TILE // 2
    low_a = move(sums[3][:half], "x", 4, 1)
    high_b = move(sums[3][half:], "x", 4, -1)
    up_hi = move(sums[2][half:], "x", 4, 1)
    down_lo = move(sums[1][:half], "x", 4, -1)
    up_lo = add(sums[2][:half], low_a).astype(BF16)
    down_hi = add(sums[1][half:], high_b).astype(BF16)
    up_lo = move(up_lo, "x", 4, 1)
    down_hi = move(down_hi, "x", 4, -1)

    keep, give = mlp_back(core.reshape(1).astype(I32), embed_grad, down_all, slope, hidden, turned)
    given = move(give, "core", 2, 1)
    both = add(keep, given).astype(BF16)
    mlp = total(lax.all_to_all(both, ("yh", "x", "yl"), 0, 0))

    half = TILE // 2
    lo = (add(sums[0][:half], up_lo) + down_lo.astype(F32)).astype(BF16)
    hi = (add(sums[0][half:], up_hi) + down_hi.astype(F32)).astype(BF16)
    y_sums = [lo[:LAB], lo[LAB:], hi[:LAB], hi[LAB:]]
    half = LAB // 2
    low_a = move(y_sums[3][:half], plane_y, 4, 1)
    high_b = move(y_sums[3][half:], plane_y, 4, -1)
    up = jnp.concatenate([add(y_sums[2][:half], low_a), y_sums[2][half:].astype(F32)], axis=0).astype(BF16)
    down = jnp.concatenate([y_sums[1][:half].astype(F32), add(y_sums[1][half:], high_b)], axis=0).astype(BF16)
    up = move(up, plane_y, 4, 1)
    down = move(down, plane_y, 4, -1)
    label_grad = add(y_sums[0], up) + down.astype(F32)
    return (label_grad, mlp[:, :units], mlp[:, units:].T)


def solution(mesh):
    cut = Mesh(np.asarray(mesh.devices).reshape(2, 4, 2, 8, 2), ("yh", "x", "core", "z", "yl"))
    wide, narrow = ("yh", "x", "core"), ("z", "yl")
    in_specs = (
        P(wide, None),
        P(wide + narrow, None),
        P(wide + narrow),
        P(wide, None),
        P(None, narrow),
        P(narrow, None),
    )
    out_specs = (P(wide + narrow, None), P(wide, narrow), P(narrow, wide))
    return jax.shard_map(step_of, mesh=cut, in_specs=in_specs, out_specs=out_specs, check_vma=False)
```

```python
from functools import partial

import jax
import jax.numpy as jnp
import numpy as np
from jax import lax
from jax.experimental import pallas as pl
from jax.experimental.pallas import tpu as pltpu
from jax.sharding import Mesh
from jax.sharding import PartitionSpec as P


CATALOG = 2812281
BF16, F32, I32 = jnp.bfloat16, jnp.float32, jnp.int32
D = 768
LAB = 128
EXTRA = 8
BLK = LAB + EXTRA
NB = 32
GRP = 4
TILE = GRP * LAB
STEPS = NB // GRP
DOCS = 512
DOWN = 384
ROWS = D // 16
REL = (0, -1, 1, 2)
NT = (((1,), (1,)), ((), ()))
TN = (((0,), (0,)), ((), ()))


def move(block, axes, size, distance):
    return lax.ppermute(block, axes, [(i, (i + distance) % size) for i in range(size)])


def add(a, b):
    return a.astype(F32) + b.astype(F32)


def total(parts):
    result = parts[0].astype(F32)
    for j in range(1, parts.shape[0]):
        result = result + parts[j].astype(F32)
    return result


def rounded(values):
    return lax.reduce_precision(values, 8, 7)


def log_expected(rank_ids, sampled):
    rank_float = rank_ids.astype(F32)
    return (
        jnp.log(F32(sampled))
        + jnp.log(jnp.log1p(1.0 / (rank_float + 1.0)))
        - jnp.log(jnp.log(F32(CATALOG) + 1.0))
    )


def fetch_labels(label_refs, rows, extras, sems):
    copies = []
    for g in range(STEPS):
        side, dx = g // 4, g % 4
        if dx < 3:
            sources = [(label_refs[side * 5 + dx], 0, GRP)]
        else:
            half = GRP // 2
            sources = [(label_refs[side * 5 + 3], 0, half), (label_refs[side * 5 + 4], half, half)]
        for n, (ref, at, size) in enumerate(sources):
            span = pl.ds(at, size)
            copies.append(
                (g, pltpu.make_async_copy(ref.at[:, pl.ds(0, LAB), :], rows[g % 2].at[span], sems.at[g, 2 * n]))
            )
            if extras is not None:
                copies.append(
                    (
                        g,
                        pltpu.make_async_copy(
                            ref.at[:, pl.ds(LAB, EXTRA), pl.ds(0, LAB)],
                            extras[g % 2].at[span],
                            sems.at[g, 2 * n + 1],
                        ),
                    )
                )
    return copies


def start_and_wait(copies, late):
    step = pl.program_id(0)
    for g in range(STEPS):

        @pl.when(step == max(g - 1 + late, 0))
        def _():
            for at, copy in copies:
                if at == g:
                    copy.start()

    for g in range(STEPS):

        @pl.when(step == g + late)
        def _():
            for at, copy in copies:
                if at == g:
                    copy.wait()


def first_kernel(*refs):
    label_refs = refs[:10]
    emb_hbm, exp_hbm, top_ref, stat_ref = refs[10:14]
    rows_a, rows_b, extras_a, extras_b, sems, emb, emb_sem = refs[14:21]
    (raw_a, raw_b, bias_a, bias_b, exp_a, exp_b, exp_sem, run_max, run_sum) = refs[21:]
    step = pl.program_id(0)
    fetch_emb = pltpu.make_async_copy(emb_hbm, emb, emb_sem)

    @pl.when(step == 0)
    def _():
        fetch_emb.start()

    start_and_wait(fetch_labels(label_refs, (rows_a, rows_b), (extras_a, extras_b), sems), 0)

    @pl.when(step == 0)
    def _():
        fetch_emb.wait()

    def put(exp_out, slot, which):
        return pltpu.make_async_copy(exp_out, exp_hbm.at[which], exp_sem.at[slot])

    def body(slot, rows, extras, raw_out, bias_out, raw_in, bias_in, exp_out):
        @pl.when(step >= 3)
        def _():
            put(exp_out, slot, step - 3).wait()

        for j in range(GRP):
            pieces = extras[j].astype(F32)
            row = pieces[0:1] + pieces[1:2] + pieces[2:3]
            bias_out[j * LAB : (j + 1) * LAB, :] = jnp.broadcast_to(row, (LAB, LAB)).T
        lhs = rows[...].reshape(TILE, D)
        for half in range(2):
            wide = slice(half * 256, (half + 1) * 256)
            raw_out[:, wide] = lax.dot_general(lhs, emb[wide, :], NT, preferred_element_type=F32)
            for h in range(2):
                cols = slice(half * 256 + h * LAB, half * 256 + (h + 1) * LAB)
                logits = raw_in[:, cols] - bias_in[...]
                old = run_max[:, cols]
                new = jnp.maximum(old, jnp.max(logits, axis=0, keepdims=True))
                exps = jnp.exp(logits - new)
                exp_out[:, cols] = exps
                run_sum[:, cols] = run_sum[:, cols] * jnp.exp(old - new) + jnp.sum(exps, axis=0, keepdims=True)
                run_max[:, cols] = new

        @pl.when(step >= 1)
        def _():
            put(exp_out, slot, step - 1).start()

        @pl.when(step == STEPS)
        def _():
            put(exp_b if slot == 0 else exp_a, 1 - slot, step - 2).wait()
            put(exp_out, slot, step - 1).wait()

    @pl.when(lax.rem(step, 2) == 0)
    def _():
        body(0, rows_a, extras_a, raw_a, bias_a, raw_b, bias_b, exp_a)

    @pl.when(lax.rem(step, 2) == 1)
    def _():
        body(1, rows_b, extras_b, raw_b, bias_b, raw_a, bias_a, exp_b)

    @pl.when(step == 0)
    def _():
        run_max[...] = jnp.full_like(run_max, -jnp.inf)
        run_sum[...] = jnp.zeros_like(run_sum)

    top_ref[0] = run_max[...]

    @pl.when(step == STEPS)
    def _():
        for j in range(4):
            stat_ref[j : j + 1, :] = run_max[:, j * 128 : (j + 1) * 128]
            stat_ref[4 + j : 5 + j, :] = run_sum[:, j * 128 : (j + 1) * 128]


def hits_kernel(base_ref, pos_ref, docs_ref, hits_ref, turned_ref):
    step = pl.program_id(0)

    @pl.when(step == 0)
    def _():
        turned_ref[...] = docs_ref[...].T

    pos = [pos_ref[k : k + 1, :] for k in range(4)]
    weights = []
    for k in range(4):
        same = [jnp.where(pos[k] == pos[n], F32(0.25), F32(0.0)) for n in range(4)]
        weights.append(same[0] + same[1] + same[2] + same[3])
    for h in range(DOCS // LAB):
        cols = slice(h * LAB, (h + 1) * LAB)
        ids = lax.broadcasted_iota(I32, (LAB, LAB), 0)

        def block(j, carry):
            base = base_ref[step * GRP + j]
            hits = jnp.zeros((LAB, LAB), F32)
            for k in (3, 2, 1, 0):
                hits = jnp.where(pos[k][:, cols] - base == ids, weights[k][:, cols], hits)
            hits_ref[0, pl.ds(pl.multiple_of(j * LAB, LAB), LAB), cols] = hits.astype(BF16)
            return carry

        lax.fori_loop(0, GRP, block, 0)


def second_kernel(*refs):
    label_refs = refs[:10]
    exp_ref, top_ref, total_ref, hits_ref, near_hbm, near_end, far_hbm, far_end, out_ref = refs[10:19]
    rows_a, rows_b, sems, grad_a, grad_b, grad_sem, acc = refs[19:]
    side = STEPS // 2
    step = pl.program_id(0)
    start_and_wait(fetch_labels(label_refs, (rows_a, rows_b), None, sems), 1)

    def put(grad, slot, home, which):
        return pltpu.make_async_copy(grad, home.at[which], grad_sem.at[slot])

    def body(slot, rows, grad_out, grad_in):
        @pl.when(step >= 2)
        def _():
            put(grad_out, slot, near_hbm, 0).wait()

        scale = jnp.exp(top_ref[0] - total_ref[...])
        for j in range(GRP):
            span = slice(j * LAB, (j + 1) * LAB)
            grad_out[span, :] = (exp_ref[0, span, :] * scale - hits_ref[0, span, :].astype(F32)).astype(BF16)
        acc[...] += lax.dot_general(
            grad_in[...], rows[...].reshape(TILE, D), TN, preferred_element_type=F32
        )

        @pl.when(step < side - 1)
        def _():
            put(grad_out, slot, near_hbm, step).start()

        @pl.when((step >= side) & (step < STEPS - 1))
        def _():
            put(grad_out, slot, far_hbm, step - side).start()

        if slot == 1:

            @pl.when(step == side - 1)
            def _():
                put(grad_out, slot, near_end, 0).start()

            @pl.when(step == STEPS - 1)
            def _():
                put(grad_out, slot, far_end, 0).start()

        @pl.when(step == STEPS)
        def _():
            put(grad_in, 1 - slot, far_end, 0).wait()

    @pl.when(lax.rem(step, 2) == 0)
    def _():
        body(0, rows_b, grad_a, grad_b)

    @pl.when(lax.rem(step, 2) == 1)
    def _():
        body(1, rows_a, grad_b, grad_a)

    @pl.when(step == 0)
    def _():
        acc[...] = jnp.zeros_like(acc)

    @pl.when(step == STEPS)
    def _():
        out_ref[...] = acc[...].astype(BF16)


def in_hbm(array):
    return pltpu.with_memory_space_constraint(array, pltpu.HBM)


def label_specs():
    return [pl.BlockSpec(memory_space=pl.ANY)] * 10


def first_pass(labels, embedding):
    return pl.pallas_call(
        first_kernel,
        out_shape=(
            jax.ShapeDtypeStruct((STEPS, TILE, DOCS), F32),
            jax.ShapeDtypeStruct((STEPS, 1, DOCS), F32),
            jax.ShapeDtypeStruct((8, 128), F32),
        ),
        grid=(STEPS + 1,),
        in_specs=label_specs() + [pl.BlockSpec(memory_space=pl.ANY)],
        out_specs=(
            pl.BlockSpec(memory_space=pl.ANY),
            pl.BlockSpec((1, 1, DOCS), lambda s: (jnp.maximum(s - 1, 0), 0, 0)),
            pl.BlockSpec((8, 128), lambda s: (0, 0)),
        ),
        scratch_shapes=[
            pltpu.VMEM((GRP, LAB, D), BF16),
            pltpu.VMEM((GRP, LAB, D), BF16),
            pltpu.VMEM((GRP, EXTRA, LAB), BF16),
            pltpu.VMEM((GRP, EXTRA, LAB), BF16),
            pltpu.SemaphoreType.DMA((STEPS, 4)),
            pltpu.VMEM((DOCS, D), BF16),
            pltpu.SemaphoreType.DMA,
            pltpu.VMEM((TILE, DOCS), F32),
            pltpu.VMEM((TILE, DOCS), F32),
            pltpu.VMEM((TILE, LAB), F32),
            pltpu.VMEM((TILE, LAB), F32),
            pltpu.VMEM((TILE, DOCS), F32),
            pltpu.VMEM((TILE, DOCS), F32),
            pltpu.SemaphoreType.DMA((2,)),
            pltpu.VMEM((1, DOCS), F32),
            pltpu.VMEM((1, DOCS), F32),
        ],
        compiler_params=pltpu.CompilerParams(
            dimension_semantics=("arbitrary",), vmem_limit_bytes=18 << 20
        ),
        cost_estimate=pl.CostEstimate(
            flops=2 * NB * LAB * DOCS * D, bytes_accessed=16 << 20, transcendentals=NB * LAB * DOCS
        ),
        name="first_pass",
    )(*labels, embedding)


def positive_hits(bases, positives, documents):
    return pl.pallas_call(
        hits_kernel,
        out_shape=(
            jax.ShapeDtypeStruct((STEPS, TILE, DOCS), BF16),
            jax.ShapeDtypeStruct((D, DOCS), BF16),
        ),
        grid_spec=pltpu.PrefetchScalarGridSpec(
            num_scalar_prefetch=1,
            grid=(STEPS,),
            in_specs=[
                pl.BlockSpec((4, DOCS), lambda s, b: (0, 0)),
                pl.BlockSpec((DOCS, D), lambda s, b: (b[NB], 0)),
            ],
            out_specs=(
                pl.BlockSpec((1, TILE, DOCS), lambda s, b: (s, 0, 0)),
                pl.BlockSpec((D, DOCS), lambda s, b: (0, 0)),
            ),
        ),
        compiler_params=pltpu.CompilerParams(dimension_semantics=("arbitrary",)),
        cost_estimate=pl.CostEstimate(
            flops=16 * NB * LAB * DOCS, bytes_accessed=4 << 20, transcendentals=0
        ),
        name="positive_hits",
    )(bases, positives, documents)


def mlp_kernel(core_ref, grad_ref, down_ref, slope_ref, hidden_ref, turned_ref, keep_ref, give_ref, both):
    units = DOWN // 2
    act_grad = lax.dot_general(grad_ref[...], down_ref[...], NT, preferred_element_type=F32)
    pre_grad = (act_grad * slope_ref[...]).astype(BF16)
    down_term = lax.dot_general(grad_ref[...], hidden_ref[...], TN, preferred_element_type=F32)
    up_term = jnp.dot(turned_ref[...], pre_grad, preferred_element_type=F32)
    for j in range(2):
        cols = slice(j * units, (j + 1) * units)
        both[j] = jnp.concatenate([up_term[:, cols], down_term[:, cols]], axis=1).astype(BF16)
    core = core_ref[0]
    for q in range(8):
        for j in range(2):
            mine = pl.multiple_of((2 * q + core) * ROWS, ROWS)
            other = pl.multiple_of((2 * q + 1 - core) * ROWS, ROWS)
            keep_ref[2 * q + j] = both[j, pl.ds(mine, ROWS), :]
            give_ref[2 * q + j] = both[j, pl.ds(other, ROWS), :]


def mlp_back(core, embed_grad, down_all, slope, hidden, turned):
    shape = jax.ShapeDtypeStruct((16, ROWS, DOWN), BF16)
    vmem = pl.BlockSpec(memory_space=pltpu.VMEM)
    return pl.pallas_call(
        mlp_kernel,
        out_shape=(shape, shape),
        in_specs=[pl.BlockSpec(memory_space=pltpu.SMEM)] + [vmem] * 5,
        out_specs=(vmem, vmem),
        scratch_shapes=[pltpu.VMEM((2, D, DOWN), BF16)],
        compiler_params=pltpu.CompilerParams(vmem_limit_bytes=24 << 20),
        cost_estimate=pl.CostEstimate(
            flops=6 * DOCS * D * DOWN, bytes_accessed=6 << 20, transcendentals=0
        ),
        name="mlp_back",
    )(core, embed_grad, down_all, slope, hidden, turned)


def second_pass(labels, exps, tops, log_total, hits):
    last = STEPS - 1
    return pl.pallas_call(
        second_kernel,
        out_shape=(
            pltpu.HBM((STEPS // 2 - 1, TILE, DOCS), BF16),
            pltpu.HBM((1, TILE, DOCS), BF16),
            pltpu.HBM((STEPS // 2 - 1, TILE, DOCS), BF16),
            pltpu.HBM((1, TILE, DOCS), BF16),
            pltpu.HBM((DOCS, D), BF16),
        ),
        grid=(STEPS + 1,),
        in_specs=label_specs()
        + [
            pl.BlockSpec((1, TILE, DOCS), lambda s: (jnp.minimum(s, last), 0, 0)),
            pl.BlockSpec((1, 1, DOCS), lambda s: (jnp.minimum(s, last), 0, 0)),
            pl.BlockSpec((1, DOCS), lambda s: (0, 0)),
            pl.BlockSpec((1, TILE, DOCS), lambda s: (jnp.minimum(s, last), 0, 0)),
        ],
        out_specs=(
            pl.BlockSpec(memory_space=pl.ANY),
            pl.BlockSpec(memory_space=pl.ANY),
            pl.BlockSpec(memory_space=pl.ANY),
            pl.BlockSpec(memory_space=pl.ANY),
            pl.BlockSpec((DOCS, D), lambda s: (0, 0)),
        ),
        scratch_shapes=[
            pltpu.VMEM((GRP, LAB, D), BF16),
            pltpu.VMEM((GRP, LAB, D), BF16),
            pltpu.SemaphoreType.DMA((STEPS, 4)),
            pltpu.VMEM((TILE, DOCS), BF16),
            pltpu.VMEM((TILE, DOCS), BF16),
            pltpu.SemaphoreType.DMA((2,)),
            pltpu.VMEM((DOCS, D), F32),
        ],
        compiler_params=pltpu.CompilerParams(
            dimension_semantics=("arbitrary",), vmem_limit_bytes=18 << 20
        ),
        cost_estimate=pl.CostEstimate(
            flops=2 * NB * LAB * DOCS * D, bytes_accessed=20 << 20, transcendentals=0
        ),
        name="second_pass",
    )(*labels, exps, tops, log_total, hits)


def spread(chunks):
    return lax.all_to_all(chunks, "z", 0, 0)


def everywhere(block):
    return spread(jnp.broadcast_to(block[None], (8,) + block.shape))


def step_of(documents, label_weight, sample_ids, positive_cols, up_weight, down_weight):
    yh, yl = lax.axis_index("yh"), lax.axis_index("yl")
    x, core, z = lax.axis_index("x"), lax.axis_index("core"), lax.axis_index("z")
    plane_y = ("yh", "yl")
    units = down_weight.shape[0]

    log_expect = log_expected(sample_ids, label_weight.shape[0] * 256)
    piece_a = rounded(log_expect)
    piece_b = rounded(log_expect - piece_a)
    piece_c = log_expect - piece_a - piece_b
    pieces = jnp.stack([piece_a, piece_b, piece_c]).astype(BF16)
    pieces = jnp.pad(pieces, ((0, EXTRA - 3), (0, D - LAB)))
    block = jnp.concatenate([label_weight, pieces], axis=0)
    y_low = move(block, plane_y, 4, 1)
    y_high = move(block, plane_y, 4, -1)
    y_far_a = move(y_low[:64], plane_y, 4, 1)
    y_far_b = move(y_high[64:], plane_y, 4, -1)
    column = jnp.concatenate([block, y_low, y_high, y_far_a, y_far_b], axis=0)
    x_low = move(column, "x", 4, 1)
    x_high = move(column, "x", 4, -1)
    c_column = move(column, "core", 2, 1)

    up_rows = up_weight.T
    mine = jnp.where(core == 0, up_rows, down_weight)
    got = move(mine, "yl", 2, 1)
    got_other = move(got, "core", 2, 1)
    up_far = jnp.where(core == 0, got, got_other)
    down_far = jnp.where(core == 0, got_other, got)
    up_all = jnp.concatenate([jnp.where(yl == 0, up_rows, up_far), jnp.where(yl == 0, up_far, up_rows)], axis=0)
    down_all = jnp.concatenate(
        [jnp.where(yl == 0, down_weight, down_far), jnp.where(yl == 0, down_far, down_weight)], axis=0
    )

    docs = lax.dynamic_slice_in_dim(documents, yl * DOCS, DOCS, 0)
    pre_act = lax.dot_general(docs, up_all, NT, preferred_element_type=F32)
    hidden, gelu_pull = jax.vjp(partial(jax.nn.gelu, approximate=False), pre_act)
    hidden = hidden.astype(BF16)
    slope = gelu_pull(jnp.ones_like(pre_act))[0]
    partial_out = jnp.dot(hidden, down_all, preferred_element_type=F32).astype(BF16)
    parts = spread(partial_out.reshape(8, DOCS // 8, D))
    own_docs = lax.dynamic_slice_in_dim(docs, z * (DOCS // 8), DOCS // 8, 0)
    own_emb = (own_docs.astype(F32) + total(parts)).astype(BF16)
    x_far_a = move(x_low[: 2 * BLK], "x", 4, 1)
    x_far_b = move(x_high[2 * BLK :], "x", 4, -1)
    c_low = move(x_low, "core", 2, 1)
    c_high = move(x_high, "core", 2, 1)
    c_far_a = move(x_far_a, "core", 2, 1)
    c_far_b = move(x_far_b, "core", 2, 1)
    embedding = everywhere(own_emb).reshape(DOCS, D)
    near = [column, x_low, x_high, x_far_a, x_far_b]
    far = [c_column, c_low, c_high, c_far_a, c_far_b]
    labels = [in_hbm(part.reshape(-1, BLK, D)) for part in near + far]

    which = jnp.arange(NB, dtype=I32)
    rel = jnp.array(REL, I32)
    b_core = core ^ (which >> 4)
    b_x = (x + rel[(which >> 2) & 3]) % 4
    b_y = (yh * 2 + yl + rel[which & 3]) % 4
    bases = (((((b_y >> 1) * 4 + b_x) * 2 + b_core) * 16) + z * 2 + (b_y & 1)) * LAB

    exps, tops, stats = first_pass(labels, in_hbm(embedding))
    all_stats = everywhere(stats)
    maxes, sums = all_stats[:, :4], all_stats[:, 4:]
    row_top = jnp.max(maxes, axis=0)
    row_total = jnp.sum(sums * jnp.exp(maxes - row_top[None]), axis=0)
    log_total = (row_top + jnp.log(row_total)).reshape(1, DOCS)
    positives = lax.dynamic_slice_in_dim(positive_cols, yl * DOCS, DOCS, 0).T
    scalars = jnp.concatenate([bases, yl.reshape(1).astype(I32)])
    hits, turned = positive_hits(scalars, positives, documents)
    near_grads, near_end, far_grads, far_end, embed_part = second_pass(labels, exps, tops, log_total, hits)

    back = spread(embed_part.reshape(8, DOCS // 8, D))
    own_grad = total(back).astype(BF16)
    embed_grad = everywhere(own_grad).reshape(DOCS, D)

    far_last = jnp.dot(far_end[0], embedding, preferred_element_type=F32).astype(BF16)
    far_last = move(far_last, "core", 2, 1)
    far_rest = jnp.dot(far_grads.reshape(-1, DOCS), embedding, preferred_element_type=F32).astype(BF16)
    far_rest = move(far_rest, "core", 2, 1)
    near_term = jnp.dot(near_end[0], embedding, preferred_element_type=F32)
    last_sum = (near_term + far_last.astype(F32)).astype(BF16)
    near_term = jnp.dot(near_grads.reshape(-1, DOCS), embedding, preferred_element_type=F32)
    rest = (near_term + far_rest.astype(F32)).astype(BF16).reshape(3, TILE, D)
    sums = [rest[0], rest[1], rest[2], last_sum]
    half = TILE // 2
    low_a = move(sums[3][:half], "x", 4, 1)
    high_b = move(sums[3][half:], "x", 4, -1)
    up_hi = move(sums[2][half:], "x", 4, 1)
    down_lo = move(sums[1][:half], "x", 4, -1)
    up_lo = add(sums[2][:half], low_a).astype(BF16)
    down_hi = add(sums[1][half:], high_b).astype(BF16)
    up_lo = move(up_lo, "x", 4, 1)
    down_hi = move(down_hi, "x", 4, -1)

    keep, give = mlp_back(core.reshape(1).astype(I32), embed_grad, down_all, slope, hidden, turned)
    given = move(give, "core", 2, 1)
    both = add(keep, given).astype(BF16)
    mlp = total(lax.all_to_all(both, ("yh", "x", "yl"), 0, 0))

    half = TILE // 2
    lo = (add(sums[0][:half], up_lo) + down_lo.astype(F32)).astype(BF16)
    hi = (add(sums[0][half:], up_hi) + down_hi.astype(F32)).astype(BF16)
    y_sums = [lo[:LAB], lo[LAB:], hi[:LAB], hi[LAB:]]
    half = LAB // 2
    low_a = move(y_sums[3][:half], plane_y, 4, 1)
    high_b = move(y_sums[3][half:], plane_y, 4, -1)
    up = jnp.concatenate([add(y_sums[2][:half], low_a), y_sums[2][half:].astype(F32)], axis=0).astype(BF16)
    down = jnp.concatenate([y_sums[1][:half].astype(F32), add(y_sums[1][half:], high_b)], axis=0).astype(BF16)
    up = move(up, plane_y, 4, 1)
    down = move(down, plane_y, 4, -1)
    label_grad = add(y_sums[0], up) + down.astype(F32)
    return (label_grad, mlp[:, :units], mlp[:, units:].T)


def solution(mesh):
    cut = Mesh(np.asarray(mesh.devices).reshape(2, 4, 2, 8, 2), ("yh", "x", "core", "z", "yl"))
    wide, narrow = ("yh", "x", "core"), ("z", "yl")
    in_specs = (
        P(wide, None),
        P(wide + narrow, None),
        P(wide + narrow),
        P(wide, None),
        P(None, narrow),
        P(narrow, None),
    )
    out_specs = (P(wide + narrow, None), P(wide, narrow), P(narrow, wide))
    return jax.shard_map(step_of, mesh=cut, in_specs=in_specs, out_specs=out_specs, check_vma=False)
```

```python
from functools import partial

import jax
import jax.numpy as jnp
import numpy as np
from jax import lax
from jax.experimental import pallas as pl
from jax.experimental.pallas import tpu as pltpu
from jax.sharding import Mesh
from jax.sharding import PartitionSpec as P


CATALOG = 2812281
BF16, F32, I32 = jnp.bfloat16, jnp.float32, jnp.int32
D = 768
LAB = 128
EXTRA = 8
BLK = LAB + EXTRA
NB = 32
GRP = 4
TILE = GRP * LAB
STEPS = NB // GRP
DOCS = 512
DOWN = 384
ROWS = D // 16
REL = (0, -1, 1, 2)
NT = (((1,), (1,)), ((), ()))
TN = (((0,), (0,)), ((), ()))


def move(block, axes, size, distance):
    return lax.ppermute(block, axes, [(i, (i + distance) % size) for i in range(size)])


def add(a, b):
    return a.astype(F32) + b.astype(F32)


def total(parts):
    result = parts[0].astype(F32)
    for j in range(1, parts.shape[0]):
        result = result + parts[j].astype(F32)
    return result


def rounded(values):
    return lax.reduce_precision(values, 8, 7)


def log_expected(rank_ids, sampled):
    rank_float = rank_ids.astype(F32)
    return (
        jnp.log(F32(sampled))
        + jnp.log(jnp.log1p(1.0 / (rank_float + 1.0)))
        - jnp.log(jnp.log(F32(CATALOG) + 1.0))
    )


def fetch_labels(label_refs, rows, extras, sems):
    copies = []
    for g in range(STEPS):
        half = GRP // 2
        sources = [(label_refs[2 * g], 0, half), (label_refs[2 * g + 1], half, half)]
        for n, (ref, at, size) in enumerate(sources):
            span = pl.ds(at, size)
            copies.append(
                (g, pltpu.make_async_copy(ref.at[:, pl.ds(0, LAB), :], rows[g % 2].at[span], sems.at[g, 2 * n]))
            )
            if extras is not None:
                copies.append(
                    (
                        g,
                        pltpu.make_async_copy(
                            ref.at[:, pl.ds(LAB, EXTRA), pl.ds(0, LAB)],
                            extras[g % 2].at[span],
                            sems.at[g, 2 * n + 1],
                        ),
                    )
                )
    return copies


def start_and_wait(copies, late):
    step = pl.program_id(0)
    for g in range(STEPS):

        @pl.when(step == max(g - 1 + late, 0))
        def _():
            for at, copy in copies:
                if at == g:
                    copy.start()

    for g in range(STEPS):

        @pl.when(step == g + late)
        def _():
            for at, copy in copies:
                if at == g:
                    copy.wait()


def first_kernel(*refs):
    label_refs = refs[:16]
    emb_hbm, exp_hbm, top_ref, stat_ref = refs[16:20]
    rows_a, rows_b, extras_a, extras_b, sems, emb, emb_sem = refs[20:27]
    (raw_a, raw_b, bias_a, bias_b, exp_a, exp_b, exp_sem, run_max, run_sum) = refs[27:]
    step = pl.program_id(0)
    fetch_emb = pltpu.make_async_copy(emb_hbm, emb, emb_sem)

    @pl.when(step == 0)
    def _():
        fetch_emb.start()

    start_and_wait(fetch_labels(label_refs, (rows_a, rows_b), (extras_a, extras_b), sems), 0)

    @pl.when(step == 0)
    def _():
        fetch_emb.wait()

    def put(exp_out, slot, which):
        return pltpu.make_async_copy(exp_out, exp_hbm.at[which], exp_sem.at[slot])

    def body(slot, rows, extras, raw_out, bias_out, raw_in, bias_in, exp_out):
        @pl.when(step >= 3)
        def _():
            put(exp_out, slot, step - 3).wait()

        for j in range(GRP):
            pieces = extras[j].astype(F32)
            row = pieces[0:1] + pieces[1:2] + pieces[2:3]
            bias_out[j * LAB : (j + 1) * LAB, :] = jnp.broadcast_to(row, (LAB, LAB)).T
        lhs = rows[...].reshape(TILE, D)
        for half in range(2):
            wide = slice(half * 256, (half + 1) * 256)
            raw_out[:, wide] = lax.dot_general(lhs, emb[wide, :], NT, preferred_element_type=F32)
            for h in range(2):
                cols = slice(half * 256 + h * LAB, half * 256 + (h + 1) * LAB)
                logits = raw_in[:, cols] - bias_in[...]
                old = run_max[:, cols]
                new = jnp.maximum(old, jnp.max(logits, axis=0, keepdims=True))
                exps = jnp.exp(logits - new)
                exp_out[:, cols] = exps
                run_sum[:, cols] = run_sum[:, cols] * jnp.exp(old - new) + jnp.sum(exps, axis=0, keepdims=True)
                run_max[:, cols] = new

        @pl.when(step >= 1)
        def _():
            put(exp_out, slot, step - 1).start()

        @pl.when(step == STEPS)
        def _():
            put(exp_b if slot == 0 else exp_a, 1 - slot, step - 2).wait()
            put(exp_out, slot, step - 1).wait()

    @pl.when(lax.rem(step, 2) == 0)
    def _():
        body(0, rows_a, extras_a, raw_a, bias_a, raw_b, bias_b, exp_a)

    @pl.when(lax.rem(step, 2) == 1)
    def _():
        body(1, rows_b, extras_b, raw_b, bias_b, raw_a, bias_a, exp_b)

    @pl.when(step == 0)
    def _():
        run_max[...] = jnp.full_like(run_max, -jnp.inf)
        run_sum[...] = jnp.zeros_like(run_sum)

    top_ref[0] = run_max[...]

    @pl.when(step == STEPS)
    def _():
        for j in range(4):
            stat_ref[j : j + 1, :] = run_max[:, j * 128 : (j + 1) * 128]
            stat_ref[4 + j : 5 + j, :] = run_sum[:, j * 128 : (j + 1) * 128]


def hits_kernel(base_ref, pos_ref, docs_ref, hits_ref, turned_ref):
    step = pl.program_id(0)

    @pl.when(step == 0)
    def _():
        turned_ref[...] = docs_ref[...].T

    pos = [pos_ref[k : k + 1, :] for k in range(4)]
    weights = []
    for k in range(4):
        same = [jnp.where(pos[k] == pos[n], F32(0.25), F32(0.0)) for n in range(4)]
        weights.append(same[0] + same[1] + same[2] + same[3])
    for h in range(DOCS // LAB):
        cols = slice(h * LAB, (h + 1) * LAB)
        ids = lax.broadcasted_iota(I32, (LAB, LAB), 0)

        def block(j, carry):
            base = base_ref[step * GRP + j]
            hits = jnp.zeros((LAB, LAB), F32)
            for k in (3, 2, 1, 0):
                hits = jnp.where(pos[k][:, cols] - base == ids, weights[k][:, cols], hits)
            hits_ref[0, pl.ds(pl.multiple_of(j * LAB, LAB), LAB), cols] = hits.astype(BF16)
            return carry

        lax.fori_loop(0, GRP, block, 0)


def second_kernel(*refs):
    label_refs = refs[:16]
    exp_ref, top_ref, total_ref, hits_ref, near_hbm, near_end, far_hbm, far_end, out_ref = refs[16:25]
    rows_a, rows_b, sems, grad_a, grad_b, grad_sem, acc = refs[25:]
    side = STEPS // 2
    step = pl.program_id(0)
    start_and_wait(fetch_labels(label_refs, (rows_a, rows_b), None, sems), 1)

    def put(grad, slot, home, which):
        return pltpu.make_async_copy(grad, home.at[which], grad_sem.at[slot])

    def body(slot, rows, grad_out, grad_in):
        @pl.when(step >= 2)
        def _():
            put(grad_out, slot, near_hbm, 0).wait()

        scale = jnp.exp(top_ref[0] - total_ref[...])
        for j in range(GRP):
            span = slice(j * LAB, (j + 1) * LAB)
            grad_out[span, :] = (exp_ref[0, span, :] * scale - hits_ref[0, span, :].astype(F32)).astype(BF16)
        acc[...] += lax.dot_general(
            grad_in[...], rows[...].reshape(TILE, D), TN, preferred_element_type=F32
        )

        @pl.when(step < side - 1)
        def _():
            put(grad_out, slot, near_hbm, step).start()

        @pl.when((step >= side) & (step < STEPS - 1))
        def _():
            put(grad_out, slot, far_hbm, step - side).start()

        if slot == 1:

            @pl.when(step == side - 1)
            def _():
                put(grad_out, slot, near_end, 0).start()

            @pl.when(step == STEPS - 1)
            def _():
                put(grad_out, slot, far_end, 0).start()

        @pl.when(step == STEPS)
        def _():
            put(grad_in, 1 - slot, far_end, 0).wait()

    @pl.when(lax.rem(step, 2) == 0)
    def _():
        body(0, rows_b, grad_a, grad_b)

    @pl.when(lax.rem(step, 2) == 1)
    def _():
        body(1, rows_a, grad_b, grad_a)

    @pl.when(step == 0)
    def _():
        acc[...] = jnp.zeros_like(acc)

    @pl.when(step == STEPS)
    def _():
        out_ref[...] = acc[...].astype(BF16)


def in_hbm(array):
    return pltpu.with_memory_space_constraint(array, pltpu.HBM)


def label_specs():
    return [pl.BlockSpec(memory_space=pl.ANY)] * 16


def first_pass(labels, embedding):
    return pl.pallas_call(
        first_kernel,
        out_shape=(
            jax.ShapeDtypeStruct((STEPS, TILE, DOCS), F32),
            jax.ShapeDtypeStruct((STEPS, 1, DOCS), F32),
            jax.ShapeDtypeStruct((8, 128), F32),
        ),
        grid=(STEPS + 1,),
        in_specs=label_specs() + [pl.BlockSpec(memory_space=pl.ANY)],
        out_specs=(
            pl.BlockSpec(memory_space=pl.ANY),
            pl.BlockSpec((1, 1, DOCS), lambda s: (jnp.maximum(s - 1, 0), 0, 0)),
            pl.BlockSpec((8, 128), lambda s: (0, 0)),
        ),
        scratch_shapes=[
            pltpu.VMEM((GRP, LAB, D), BF16),
            pltpu.VMEM((GRP, LAB, D), BF16),
            pltpu.VMEM((GRP, EXTRA, LAB), BF16),
            pltpu.VMEM((GRP, EXTRA, LAB), BF16),
            pltpu.SemaphoreType.DMA((STEPS, 4)),
            pltpu.VMEM((DOCS, D), BF16),
            pltpu.SemaphoreType.DMA,
            pltpu.VMEM((TILE, DOCS), F32),
            pltpu.VMEM((TILE, DOCS), F32),
            pltpu.VMEM((TILE, LAB), F32),
            pltpu.VMEM((TILE, LAB), F32),
            pltpu.VMEM((TILE, DOCS), F32),
            pltpu.VMEM((TILE, DOCS), F32),
            pltpu.SemaphoreType.DMA((2,)),
            pltpu.VMEM((1, DOCS), F32),
            pltpu.VMEM((1, DOCS), F32),
        ],
        compiler_params=pltpu.CompilerParams(
            dimension_semantics=("arbitrary",), vmem_limit_bytes=18 << 20
        ),
        cost_estimate=pl.CostEstimate(
            flops=2 * NB * LAB * DOCS * D, bytes_accessed=16 << 20, transcendentals=NB * LAB * DOCS
        ),
        name="first_pass",
    )(*labels, embedding)


def positive_hits(bases, positives, documents):
    return pl.pallas_call(
        hits_kernel,
        out_shape=(
            jax.ShapeDtypeStruct((STEPS, TILE, DOCS), BF16),
            jax.ShapeDtypeStruct((D, DOCS), BF16),
        ),
        grid_spec=pltpu.PrefetchScalarGridSpec(
            num_scalar_prefetch=1,
            grid=(STEPS,),
            in_specs=[
                pl.BlockSpec((4, DOCS), lambda s, b: (0, 0)),
                pl.BlockSpec((DOCS, D), lambda s, b: (b[NB], 0)),
            ],
            out_specs=(
                pl.BlockSpec((1, TILE, DOCS), lambda s, b: (s, 0, 0)),
                pl.BlockSpec((D, DOCS), lambda s, b: (0, 0)),
            ),
        ),
        compiler_params=pltpu.CompilerParams(dimension_semantics=("arbitrary",)),
        cost_estimate=pl.CostEstimate(
            flops=16 * NB * LAB * DOCS, bytes_accessed=4 << 20, transcendentals=0
        ),
        name="positive_hits",
    )(bases, positives, documents)


def mlp_kernel(core_ref, grad_ref, down_ref, slope_ref, hidden_ref, turned_ref, keep_ref, give_ref, both):
    units = DOWN // 2
    act_grad = lax.dot_general(grad_ref[...], down_ref[...], NT, preferred_element_type=F32)
    pre_grad = (act_grad * slope_ref[...]).astype(BF16)
    down_term = lax.dot_general(grad_ref[...], hidden_ref[...], TN, preferred_element_type=F32)
    up_term = jnp.dot(turned_ref[...], pre_grad, preferred_element_type=F32)
    for j in range(2):
        cols = slice(j * units, (j + 1) * units)
        both[j] = jnp.concatenate([up_term[:, cols], down_term[:, cols]], axis=1).astype(BF16)
    core = core_ref[0]
    for q in range(8):
        for j in range(2):
            mine = pl.multiple_of((2 * q + core) * ROWS, ROWS)
            other = pl.multiple_of((2 * q + 1 - core) * ROWS, ROWS)
            keep_ref[2 * q + j] = both[j, pl.ds(mine, ROWS), :]
            give_ref[2 * q + j] = both[j, pl.ds(other, ROWS), :]


def mlp_back(core, embed_grad, down_all, slope, hidden, turned):
    shape = jax.ShapeDtypeStruct((16, ROWS, DOWN), BF16)
    vmem = pl.BlockSpec(memory_space=pltpu.VMEM)
    return pl.pallas_call(
        mlp_kernel,
        out_shape=(shape, shape),
        in_specs=[pl.BlockSpec(memory_space=pltpu.SMEM)] + [vmem] * 5,
        out_specs=(vmem, vmem),
        scratch_shapes=[pltpu.VMEM((2, D, DOWN), BF16)],
        compiler_params=pltpu.CompilerParams(vmem_limit_bytes=24 << 20),
        cost_estimate=pl.CostEstimate(
            flops=6 * DOCS * D * DOWN, bytes_accessed=6 << 20, transcendentals=0
        ),
        name="mlp_back",
    )(core, embed_grad, down_all, slope, hidden, turned)


def second_pass(labels, exps, tops, log_total, hits):
    last = STEPS - 1
    return pl.pallas_call(
        second_kernel,
        out_shape=(
            pltpu.HBM((STEPS // 2 - 1, TILE, DOCS), BF16),
            pltpu.HBM((1, TILE, DOCS), BF16),
            pltpu.HBM((STEPS // 2 - 1, TILE, DOCS), BF16),
            pltpu.HBM((1, TILE, DOCS), BF16),
            pltpu.HBM((DOCS, D), BF16),
        ),
        grid=(STEPS + 1,),
        in_specs=label_specs()
        + [
            pl.BlockSpec((1, TILE, DOCS), lambda s: (jnp.minimum(s, last), 0, 0)),
            pl.BlockSpec((1, 1, DOCS), lambda s: (jnp.minimum(s, last), 0, 0)),
            pl.BlockSpec((1, DOCS), lambda s: (0, 0)),
            pl.BlockSpec((1, TILE, DOCS), lambda s: (jnp.minimum(s, last), 0, 0)),
        ],
        out_specs=(
            pl.BlockSpec(memory_space=pl.ANY),
            pl.BlockSpec(memory_space=pl.ANY),
            pl.BlockSpec(memory_space=pl.ANY),
            pl.BlockSpec(memory_space=pl.ANY),
            pl.BlockSpec((DOCS, D), lambda s: (0, 0)),
        ),
        scratch_shapes=[
            pltpu.VMEM((GRP, LAB, D), BF16),
            pltpu.VMEM((GRP, LAB, D), BF16),
            pltpu.SemaphoreType.DMA((STEPS, 4)),
            pltpu.VMEM((TILE, DOCS), BF16),
            pltpu.VMEM((TILE, DOCS), BF16),
            pltpu.SemaphoreType.DMA((2,)),
            pltpu.VMEM((DOCS, D), F32),
        ],
        compiler_params=pltpu.CompilerParams(
            dimension_semantics=("arbitrary",), vmem_limit_bytes=18 << 20
        ),
        cost_estimate=pl.CostEstimate(
            flops=2 * NB * LAB * DOCS * D, bytes_accessed=20 << 20, transcendentals=0
        ),
        name="second_pass",
    )(*labels, exps, tops, log_total, hits)


def spread(chunks):
    return lax.all_to_all(chunks, "z", 0, 0)


def everywhere(block):
    return spread(jnp.broadcast_to(block[None], (8,) + block.shape))


def step_of(documents, label_weight, sample_ids, positive_cols, up_weight, down_weight):
    yh, yl = lax.axis_index("yh"), lax.axis_index("yl")
    x, core, z = lax.axis_index("x"), lax.axis_index("core"), lax.axis_index("z")
    plane_y = ("yh", "yl")
    units = down_weight.shape[0]

    log_expect = log_expected(sample_ids, label_weight.shape[0] * 256)
    piece_a = rounded(log_expect)
    piece_b = rounded(log_expect - piece_a)
    piece_c = log_expect - piece_a - piece_b
    pieces = jnp.stack([piece_a, piece_b, piece_c]).astype(BF16)
    pieces = jnp.pad(pieces, ((0, EXTRA - 3), (0, D - LAB)))
    block = jnp.concatenate([label_weight, pieces], axis=0)
    y_low = move(block, plane_y, 4, 1)
    y_high = move(block, plane_y, 4, -1)
    y_far_a = move(y_low[:64], plane_y, 4, 1)
    y_far_b = move(y_high[64:], plane_y, 4, -1)
    col_a = jnp.concatenate([block, y_low], axis=0)
    col_b = jnp.concatenate([y_high, y_far_a, y_far_b], axis=0)
    low_a = move(col_a, "x", 4, 1)
    high_a = move(col_a, "x", 4, -1)
    low_b = move(col_b, "x", 4, 1)
    high_b = move(col_b, "x", 4, -1)
    far_a = move(low_a, "x", 4, 1)
    far_b = move(high_b, "x", 4, -1)
    near = [col_a, col_b, low_a, low_b, high_a, high_b, far_a, far_b]
    far = [move(part, "core", 2, 1) for part in near[:2]]
    far += [move(part, "core", 2, 1) for part in near[2:]]

    up_rows = up_weight.T
    mine = jnp.where(core == 0, up_rows, down_weight)
    got = move(mine, "yl", 2, 1)
    got_other = move(got, "core", 2, 1)
    up_far = jnp.where(core == 0, got, got_other)
    down_far = jnp.where(core == 0, got_other, got)
    up_all = jnp.concatenate([jnp.where(yl == 0, up_rows, up_far), jnp.where(yl == 0, up_far, up_rows)], axis=0)
    down_all = jnp.concatenate(
        [jnp.where(yl == 0, down_weight, down_far), jnp.where(yl == 0, down_far, down_weight)], axis=0
    )

    docs = lax.dynamic_slice_in_dim(documents, yl * DOCS, DOCS, 0)
    pre_act = lax.dot_general(docs, up_all, NT, preferred_element_type=F32)
    hidden, gelu_pull = jax.vjp(partial(jax.nn.gelu, approximate=False), pre_act)
    hidden = hidden.astype(BF16)
    slope = gelu_pull(jnp.ones_like(pre_act))[0]
    partial_out = jnp.dot(hidden, down_all, preferred_element_type=F32).astype(BF16)
    parts = spread(partial_out.reshape(8, DOCS // 8, D))
    own_docs = lax.dynamic_slice_in_dim(docs, z * (DOCS // 8), DOCS // 8, 0)
    own_emb = (own_docs.astype(F32) + total(parts)).astype(BF16)
    embedding = everywhere(own_emb).reshape(DOCS, D)
    labels = [in_hbm(part.reshape(-1, BLK, D)) for part in near + far]

    which = jnp.arange(NB, dtype=I32)
    rel = jnp.array(REL, I32)
    b_core = core ^ (which >> 4)
    b_x = (x + rel[(which >> 2) & 3]) % 4
    b_y = (yh * 2 + yl + rel[which & 3]) % 4
    bases = (((((b_y >> 1) * 4 + b_x) * 2 + b_core) * 16) + z * 2 + (b_y & 1)) * LAB

    exps, tops, stats = first_pass(labels, in_hbm(embedding))
    all_stats = everywhere(stats)
    maxes, sums = all_stats[:, :4], all_stats[:, 4:]
    row_top = jnp.max(maxes, axis=0)
    row_total = jnp.sum(sums * jnp.exp(maxes - row_top[None]), axis=0)
    log_total = (row_top + jnp.log(row_total)).reshape(1, DOCS)
    positives = lax.dynamic_slice_in_dim(positive_cols, yl * DOCS, DOCS, 0).T
    scalars = jnp.concatenate([bases, yl.reshape(1).astype(I32)])
    hits, turned = positive_hits(scalars, positives, documents)
    near_grads, near_end, far_grads, far_end, embed_part = second_pass(labels, exps, tops, log_total, hits)

    back = spread(embed_part.reshape(8, DOCS // 8, D))
    own_grad = total(back).astype(BF16)
    embed_grad = everywhere(own_grad).reshape(DOCS, D)

    far_last = jnp.dot(far_end[0], embedding, preferred_element_type=F32).astype(BF16)
    far_last = move(far_last, "core", 2, 1)
    far_rest = jnp.dot(far_grads.reshape(-1, DOCS), embedding, preferred_element_type=F32).astype(BF16)
    far_rest = move(far_rest, "core", 2, 1)
    near_term = jnp.dot(near_end[0], embedding, preferred_element_type=F32)
    last_sum = (near_term + far_last.astype(F32)).astype(BF16)
    near_term = jnp.dot(near_grads.reshape(-1, DOCS), embedding, preferred_element_type=F32)
    rest = (near_term + far_rest.astype(F32)).astype(BF16).reshape(3, TILE, D)
    sums = [rest[0], rest[1], rest[2], last_sum]
    half = TILE // 2
    low_a = move(sums[3][:half], "x", 4, 1)
    high_b = move(sums[3][half:], "x", 4, -1)
    up_hi = move(sums[2][half:], "x", 4, 1)
    down_lo = move(sums[1][:half], "x", 4, -1)
    up_lo = add(sums[2][:half], low_a).astype(BF16)
    down_hi = add(sums[1][half:], high_b).astype(BF16)
    up_lo, down_hi = lax.optimization_barrier((up_lo, down_hi))
    up_lo = move(up_lo, "x", 4, 1)
    down_hi = move(down_hi, "x", 4, -1)

    keep, give = mlp_back(core.reshape(1).astype(I32), embed_grad, down_all, slope, hidden, turned)
    given = move(give, "core", 2, 1)
    both = add(keep, given).astype(BF16)
    mlp = total(lax.all_to_all(both, ("yh", "x", "yl"), 0, 0))

    half = TILE // 2
    lo = (add(sums[0][:half], up_lo) + down_lo.astype(F32)).astype(BF16)
    hi = (add(sums[0][half:], up_hi) + down_hi.astype(F32)).astype(BF16)
    y_sums = [lo[:LAB], lo[LAB:], hi[:LAB], hi[LAB:]]
    half = LAB // 2
    low_a = move(y_sums[3][:half], plane_y, 4, 1)
    high_b = move(y_sums[3][half:], plane_y, 4, -1)
    up = jnp.concatenate([add(y_sums[2][:half], low_a), y_sums[2][half:].astype(F32)], axis=0).astype(BF16)
    down = jnp.concatenate([y_sums[1][:half].astype(F32), add(y_sums[1][half:], high_b)], axis=0).astype(BF16)
    up = move(up, plane_y, 4, 1)
    down = move(down, plane_y, 4, -1)
    label_grad = add(y_sums[0], up) + down.astype(F32)
    return (label_grad, mlp[:, :units], mlp[:, units:].T)


def solution(mesh):
    cut = Mesh(np.asarray(mesh.devices).reshape(2, 4, 2, 8, 2), ("yh", "x", "core", "z", "yl"))
    wide, narrow = ("yh", "x", "core"), ("z", "yl")
    in_specs = (
        P(wide, None),
        P(wide + narrow, None),
        P(wide + narrow),
        P(wide, None),
        P(None, narrow),
        P(narrow, None),
    )
    out_specs = (P(wide + narrow, None), P(wide, narrow), P(narrow, wide))
    return jax.shard_map(step_of, mesh=cut, in_specs=in_specs, out_specs=out_specs, check_vma=False)
```

```python
from functools import partial

import jax
import jax.numpy as jnp
import numpy as np
from jax import lax
from jax.experimental import pallas as pl
from jax.experimental.pallas import tpu as pltpu
from jax.sharding import Mesh
from jax.sharding import PartitionSpec as P


CATALOG = 2812281
BF16, F32, I32 = jnp.bfloat16, jnp.float32, jnp.int32
D = 768
LAB = 128
EXTRA = 8
BLK = LAB + EXTRA
NB = 32
GRP = 4
TILE = GRP * LAB
STEPS = NB // GRP
DOCS = 512
DOWN = 384
ROWS = D // 16
REL = (0, -1, 1, 2)
NT = (((1,), (1,)), ((), ()))
TN = (((0,), (0,)), ((), ()))


def move(block, axes, size, distance):
    return lax.ppermute(block, axes, [(i, (i + distance) % size) for i in range(size)])


def add(a, b):
    return a.astype(F32) + b.astype(F32)


def total(parts):
    result = parts[0].astype(F32)
    for j in range(1, parts.shape[0]):
        result = result + parts[j].astype(F32)
    return result


def rounded(values):
    return lax.reduce_precision(values, 8, 7)


def log_expected(rank_ids, sampled):
    rank_float = rank_ids.astype(F32)
    return (
        jnp.log(F32(sampled))
        + jnp.log(jnp.log1p(1.0 / (rank_float + 1.0)))
        - jnp.log(jnp.log(F32(CATALOG) + 1.0))
    )


def fetch_labels(label_refs, rows, extras, sems):
    copies = []
    for g in range(STEPS):
        side, dx = g // 4, g % 4
        if dx < 3:
            sources = [(label_refs[side * 5 + dx], 0, GRP)]
        else:
            half = GRP // 2
            sources = [(label_refs[side * 5 + 3], 0, half), (label_refs[side * 5 + 4], half, half)]
        for n, (ref, at, size) in enumerate(sources):
            span = pl.ds(at, size)
            copies.append(
                (g, pltpu.make_async_copy(ref.at[:, pl.ds(0, LAB), :], rows[g % 2].at[span], sems.at[g, 2 * n]))
            )
            if extras is not None:
                copies.append(
                    (
                        g,
                        pltpu.make_async_copy(
                            ref.at[:, pl.ds(LAB, EXTRA), pl.ds(0, LAB)],
                            extras[g % 2].at[span],
                            sems.at[g, 2 * n + 1],
                        ),
                    )
                )
    return copies


def start_and_wait(copies, late):
    step = pl.program_id(0)
    for g in range(STEPS):

        @pl.when(step == max(g - 1 + late, 0))
        def _():
            for at, copy in copies:
                if at == g:
                    copy.start()

    for g in range(STEPS):

        @pl.when(step == g + late)
        def _():
            for at, copy in copies:
                if at == g:
                    copy.wait()


def first_kernel(*refs):
    label_refs = refs[:10]
    emb_hbm, exp_hbm, top_ref, stat_ref = refs[10:14]
    rows_a, rows_b, extras_a, extras_b, sems, emb, emb_sem = refs[14:21]
    (raw_a, raw_b, bias_a, bias_b, exp_a, exp_b, exp_sem, run_max, run_sum) = refs[21:]
    step = pl.program_id(0)
    fetch_emb = pltpu.make_async_copy(emb_hbm, emb, emb_sem)

    @pl.when(step == 0)
    def _():
        fetch_emb.start()

    start_and_wait(fetch_labels(label_refs, (rows_a, rows_b), (extras_a, extras_b), sems), 0)

    @pl.when(step == 0)
    def _():
        fetch_emb.wait()

    def put(exp_out, slot, which):
        return pltpu.make_async_copy(exp_out, exp_hbm.at[which], exp_sem.at[slot])

    def body(slot, rows, extras, raw_out, bias_out, raw_in, bias_in, exp_out):
        @pl.when(step >= 3)
        def _():
            put(exp_out, slot, step - 3).wait()

        for j in range(GRP):
            pieces = extras[j].astype(F32)
            row = pieces[0:1] + pieces[1:2] + pieces[2:3]
            bias_out[j * LAB : (j + 1) * LAB, :] = jnp.broadcast_to(row, (LAB, LAB)).T
        lhs = rows[...].reshape(TILE, D)
        for half in range(2):
            wide = slice(half * 256, (half + 1) * 256)
            raw_out[:, wide] = lax.dot_general(lhs, emb[wide, :], NT, preferred_element_type=F32)
            for h in range(2):
                cols = slice(half * 256 + h * LAB, half * 256 + (h + 1) * LAB)
                logits = raw_in[:, cols] - bias_in[...]
                old = run_max[:, cols]
                new = jnp.maximum(old, jnp.max(logits, axis=0, keepdims=True))
                exps = jnp.exp(logits - new)
                exp_out[:, cols] = exps
                run_sum[:, cols] = run_sum[:, cols] * jnp.exp(old - new) + jnp.sum(exps, axis=0, keepdims=True)
                run_max[:, cols] = new

        @pl.when(step >= 1)
        def _():
            put(exp_out, slot, step - 1).start()

        @pl.when(step == STEPS)
        def _():
            put(exp_b if slot == 0 else exp_a, 1 - slot, step - 2).wait()
            put(exp_out, slot, step - 1).wait()

    @pl.when(lax.rem(step, 2) == 0)
    def _():
        body(0, rows_a, extras_a, raw_a, bias_a, raw_b, bias_b, exp_a)

    @pl.when(lax.rem(step, 2) == 1)
    def _():
        body(1, rows_b, extras_b, raw_b, bias_b, raw_a, bias_a, exp_b)

    @pl.when(step == 0)
    def _():
        run_max[...] = jnp.full_like(run_max, -jnp.inf)
        run_sum[...] = jnp.zeros_like(run_sum)

    top_ref[0] = run_max[...]

    @pl.when(step == STEPS)
    def _():
        for j in range(4):
            stat_ref[j : j + 1, :] = run_max[:, j * 128 : (j + 1) * 128]
            stat_ref[4 + j : 5 + j, :] = run_sum[:, j * 128 : (j + 1) * 128]


def hits_kernel(base_ref, pos_ref, docs_ref, hits_ref, turned_ref):
    step = pl.program_id(0)

    @pl.when(step == 0)
    def _():
        turned_ref[...] = docs_ref[...].T

    pos = [pos_ref[k : k + 1, :] for k in range(4)]
    weights = []
    for k in range(4):
        same = [jnp.where(pos[k] == pos[n], F32(0.25), F32(0.0)) for n in range(4)]
        weights.append(same[0] + same[1] + same[2] + same[3])
    for h in range(DOCS // LAB):
        cols = slice(h * LAB, (h + 1) * LAB)
        ids = lax.broadcasted_iota(I32, (LAB, LAB), 0)

        def block(j, carry):
            base = base_ref[step * GRP + j]
            hits = jnp.zeros((LAB, LAB), F32)
            for k in (3, 2, 1, 0):
                hits = jnp.where(pos[k][:, cols] - base == ids, weights[k][:, cols], hits)
            hits_ref[0, pl.ds(pl.multiple_of(j * LAB, LAB), LAB), cols] = hits.astype(BF16)
            return carry

        lax.fori_loop(0, GRP, block, 0)


def second_kernel(*refs):
    label_refs = refs[:10]
    exp_ref, top_ref, total_ref, hits_ref, near_hbm, near_end, far_hbm, far_end, out_ref = refs[10:19]
    rows_ref, sems, grads, grad_sem, acc = refs[19:]
    side = STEPS // 2
    step = pl.program_id(0)
    slot = lax.rem(step, 2)
    start_and_wait(fetch_labels(label_refs, (rows_ref.at[0], rows_ref.at[1]), None, sems), 0)

    def put(at, home, which):
        return pltpu.make_async_copy(grads.at[at], home.at[which], grad_sem.at[at])

    @pl.when(step == 0)
    def _():
        acc[...] = jnp.zeros_like(acc)

    @pl.when(step >= 2)
    def _():
        put(slot, near_hbm, 0).wait()

    scale = jnp.exp(top_ref[0] - total_ref[...])
    for j in range(GRP):
        span = slice(j * LAB, (j + 1) * LAB)
        grads[slot, span, :] = (exp_ref[0, span, :] * scale - hits_ref[0, span, :].astype(F32)).astype(BF16)

    rows = rows_ref[slot].reshape(TILE, D)
    acc[...] += lax.dot_general(grads[slot], rows, TN, preferred_element_type=F32)

    @pl.when(step < side - 1)
    def _():
        put(slot, near_hbm, step).start()

    @pl.when((step >= side) & (step < STEPS - 1))
    def _():
        put(slot, far_hbm, step - side).start()

    @pl.when(step == side - 1)
    def _():
        put(slot, near_end, 0).start()

    @pl.when(step == STEPS - 1)
    def _():
        put(slot, far_end, 0).start()
        put(1 - slot, far_hbm, 0).wait()
        put(slot, far_end, 0).wait()
        out_ref[...] = acc[...].astype(BF16)


def in_hbm(array):
    return pltpu.with_memory_space_constraint(array, pltpu.HBM)


def label_specs():
    return [pl.BlockSpec(memory_space=pl.ANY)] * 10


def first_pass(labels, embedding):
    return pl.pallas_call(
        first_kernel,
        out_shape=(
            jax.ShapeDtypeStruct((STEPS, TILE, DOCS), F32),
            jax.ShapeDtypeStruct((STEPS, 1, DOCS), F32),
            jax.ShapeDtypeStruct((8, 128), F32),
        ),
        grid=(STEPS + 1,),
        in_specs=label_specs() + [pl.BlockSpec(memory_space=pl.ANY)],
        out_specs=(
            pl.BlockSpec(memory_space=pl.ANY),
            pl.BlockSpec((1, 1, DOCS), lambda s: (jnp.maximum(s - 1, 0), 0, 0)),
            pl.BlockSpec((8, 128), lambda s: (0, 0)),
        ),
        scratch_shapes=[
            pltpu.VMEM((GRP, LAB, D), BF16),
            pltpu.VMEM((GRP, LAB, D), BF16),
            pltpu.VMEM((GRP, EXTRA, LAB), BF16),
            pltpu.VMEM((GRP, EXTRA, LAB), BF16),
            pltpu.SemaphoreType.DMA((STEPS, 4)),
            pltpu.VMEM((DOCS, D), BF16),
            pltpu.SemaphoreType.DMA,
            pltpu.VMEM((TILE, DOCS), F32),
            pltpu.VMEM((TILE, DOCS), F32),
            pltpu.VMEM((TILE, LAB), F32),
            pltpu.VMEM((TILE, LAB), F32),
            pltpu.VMEM((TILE, DOCS), F32),
            pltpu.VMEM((TILE, DOCS), F32),
            pltpu.SemaphoreType.DMA((2,)),
            pltpu.VMEM((1, DOCS), F32),
            pltpu.VMEM((1, DOCS), F32),
        ],
        compiler_params=pltpu.CompilerParams(
            dimension_semantics=("arbitrary",), vmem_limit_bytes=18 << 20
        ),
        cost_estimate=pl.CostEstimate(
            flops=2 * NB * LAB * DOCS * D, bytes_accessed=16 << 20, transcendentals=NB * LAB * DOCS
        ),
        name="first_pass",
    )(*labels, embedding)


def positive_hits(bases, positives, documents):
    return pl.pallas_call(
        hits_kernel,
        out_shape=(
            jax.ShapeDtypeStruct((STEPS, TILE, DOCS), BF16),
            jax.ShapeDtypeStruct((D, DOCS), BF16),
        ),
        grid_spec=pltpu.PrefetchScalarGridSpec(
            num_scalar_prefetch=1,
            grid=(STEPS,),
            in_specs=[
                pl.BlockSpec((4, DOCS), lambda s, b: (0, 0)),
                pl.BlockSpec((DOCS, D), lambda s, b: (b[NB], 0)),
            ],
            out_specs=(
                pl.BlockSpec((1, TILE, DOCS), lambda s, b: (s, 0, 0)),
                pl.BlockSpec((D, DOCS), lambda s, b: (0, 0)),
            ),
        ),
        compiler_params=pltpu.CompilerParams(dimension_semantics=("arbitrary",)),
        cost_estimate=pl.CostEstimate(
            flops=16 * NB * LAB * DOCS, bytes_accessed=4 << 20, transcendentals=0
        ),
        name="positive_hits",
    )(bases, positives, documents)


def mlp_kernel(core_ref, grad_ref, down_ref, slope_ref, hidden_ref, turned_ref, keep_ref, give_ref, both):
    units = DOWN // 2
    act_grad = lax.dot_general(grad_ref[...], down_ref[...], NT, preferred_element_type=F32)
    pre_grad = (act_grad * slope_ref[...]).astype(BF16)
    down_term = lax.dot_general(grad_ref[...], hidden_ref[...], TN, preferred_element_type=F32)
    up_term = jnp.dot(turned_ref[...], pre_grad, preferred_element_type=F32)
    for j in range(2):
        cols = slice(j * units, (j + 1) * units)
        both[j] = jnp.concatenate([up_term[:, cols], down_term[:, cols]], axis=1).astype(BF16)
    core = core_ref[0]
    for q in range(8):
        for j in range(2):
            mine = pl.multiple_of((2 * q + core) * ROWS, ROWS)
            other = pl.multiple_of((2 * q + 1 - core) * ROWS, ROWS)
            keep_ref[2 * q + j] = both[j, pl.ds(mine, ROWS), :]
            give_ref[2 * q + j] = both[j, pl.ds(other, ROWS), :]


def mlp_back(core, embed_grad, down_all, slope, hidden, turned):
    shape = jax.ShapeDtypeStruct((16, ROWS, DOWN), BF16)
    vmem = pl.BlockSpec(memory_space=pltpu.VMEM)
    return pl.pallas_call(
        mlp_kernel,
        out_shape=(shape, shape),
        in_specs=[pl.BlockSpec(memory_space=pltpu.SMEM)] + [vmem] * 5,
        out_specs=(vmem, vmem),
        scratch_shapes=[pltpu.VMEM((2, D, DOWN), BF16)],
        compiler_params=pltpu.CompilerParams(vmem_limit_bytes=24 << 20),
        cost_estimate=pl.CostEstimate(
            flops=6 * DOCS * D * DOWN, bytes_accessed=6 << 20, transcendentals=0
        ),
        name="mlp_back",
    )(core, embed_grad, down_all, slope, hidden, turned)


def second_pass(labels, exps, tops, log_total, hits):
    return pl.pallas_call(
        second_kernel,
        out_shape=(
            pltpu.HBM((STEPS // 2 - 1, TILE, DOCS), BF16),
            pltpu.HBM((1, TILE, DOCS), BF16),
            pltpu.HBM((STEPS // 2 - 1, TILE, DOCS), BF16),
            pltpu.HBM((1, TILE, DOCS), BF16),
            pltpu.HBM((DOCS, D), BF16),
        ),
        grid=(STEPS,),
        in_specs=label_specs()
        + [
            pl.BlockSpec((1, TILE, DOCS), lambda s: (s, 0, 0)),
            pl.BlockSpec((1, 1, DOCS), lambda s: (s, 0, 0)),
            pl.BlockSpec((1, DOCS), lambda s: (0, 0)),
            pl.BlockSpec((1, TILE, DOCS), lambda s: (s, 0, 0)),
        ],
        out_specs=(
            pl.BlockSpec(memory_space=pl.ANY),
            pl.BlockSpec(memory_space=pl.ANY),
            pl.BlockSpec(memory_space=pl.ANY),
            pl.BlockSpec(memory_space=pl.ANY),
            pl.BlockSpec((DOCS, D), lambda s: (0, 0)),
        ),
        scratch_shapes=[
            pltpu.VMEM((2, GRP, LAB, D), BF16),
            pltpu.SemaphoreType.DMA((STEPS, 4)),
            pltpu.VMEM((2, TILE, DOCS), BF16),
            pltpu.SemaphoreType.DMA((2,)),
            pltpu.VMEM((DOCS, D), F32),
        ],
        compiler_params=pltpu.CompilerParams(
            dimension_semantics=("arbitrary",), vmem_limit_bytes=18 << 20
        ),
        cost_estimate=pl.CostEstimate(
            flops=2 * NB * LAB * DOCS * D, bytes_accessed=20 << 20, transcendentals=0
        ),
        name="second_pass",
    )(*labels, exps, tops, log_total, hits)


def spread(chunks):
    return lax.all_to_all(chunks, "z", 0, 0)


def everywhere(block):
    return spread(jnp.broadcast_to(block[None], (8,) + block.shape))


def step_of(documents, label_weight, sample_ids, positive_cols, up_weight, down_weight):
    yh, yl = lax.axis_index("yh"), lax.axis_index("yl")
    x, core, z = lax.axis_index("x"), lax.axis_index("core"), lax.axis_index("z")
    plane_y = ("yh", "yl")
    units = down_weight.shape[0]

    log_expect = log_expected(sample_ids, label_weight.shape[0] * 256)
    piece_a = rounded(log_expect)
    piece_b = rounded(log_expect - piece_a)
    piece_c = log_expect - piece_a - piece_b
    pieces = jnp.stack([piece_a, piece_b, piece_c]).astype(BF16)
    pieces = jnp.pad(pieces, ((0, EXTRA - 3), (0, D - LAB)))
    block = jnp.concatenate([label_weight, pieces], axis=0)
    y_low = move(block, plane_y, 4, 1)
    y_high = move(block, plane_y, 4, -1)
    y_far_a = move(y_low[:64], plane_y, 4, 1)
    y_far_b = move(y_high[64:], plane_y, 4, -1)
    column = jnp.concatenate([block, y_low, y_high, y_far_a, y_far_b], axis=0)
    x_low = move(column, "x", 4, 1)
    x_high = move(column, "x", 4, -1)
    x_far_a = move(x_low[: 2 * BLK], "x", 4, 1)
    x_far_b = move(x_high[2 * BLK :], "x", 4, -1)
    near = [column, x_low, x_high, x_far_a, x_far_b]
    far = [move(column, "core", 2, 1)]
    far += [move(part, "core", 2, 1) for part in near[1:]]

    up_rows = up_weight.T
    mine = jnp.where(core == 0, up_rows, down_weight)
    got = move(mine, "yl", 2, 1)
    got_other = move(got, "core", 2, 1)
    up_far = jnp.where(core == 0, got, got_other)
    down_far = jnp.where(core == 0, got_other, got)
    up_all = jnp.concatenate([jnp.where(yl == 0, up_rows, up_far), jnp.where(yl == 0, up_far, up_rows)], axis=0)
    down_all = jnp.concatenate(
        [jnp.where(yl == 0, down_weight, down_far), jnp.where(yl == 0, down_far, down_weight)], axis=0
    )

    docs = lax.dynamic_slice_in_dim(documents, yl * DOCS, DOCS, 0)
    pre_act = lax.dot_general(docs, up_all, NT, preferred_element_type=F32)
    hidden, gelu_pull = jax.vjp(partial(jax.nn.gelu, approximate=False), pre_act)
    hidden = hidden.astype(BF16)
    slope = gelu_pull(jnp.ones_like(pre_act))[0]
    partial_out = jnp.dot(hidden, down_all, preferred_element_type=F32).astype(BF16)
    parts = spread(partial_out.reshape(8, DOCS // 8, D))
    own_docs = lax.dynamic_slice_in_dim(docs, z * (DOCS // 8), DOCS // 8, 0)
    own_emb = (own_docs.astype(F32) + total(parts)).astype(BF16)
    embedding = everywhere(own_emb).reshape(DOCS, D)
    labels = [in_hbm(part.reshape(-1, BLK, D)) for part in near + far]

    which = jnp.arange(NB, dtype=I32)
    rel = jnp.array(REL, I32)
    b_core = core ^ (which >> 4)
    b_x = (x + rel[(which >> 2) & 3]) % 4
    b_y = (yh * 2 + yl + rel[which & 3]) % 4
    bases = (((((b_y >> 1) * 4 + b_x) * 2 + b_core) * 16) + z * 2 + (b_y & 1)) * LAB

    exps, tops, stats = first_pass(labels, in_hbm(embedding))
    all_stats = everywhere(stats)
    maxes, sums = all_stats[:, :4], all_stats[:, 4:]
    row_top = jnp.max(maxes, axis=0)
    row_total = jnp.sum(sums * jnp.exp(maxes - row_top[None]), axis=0)
    log_total = (row_top + jnp.log(row_total)).reshape(1, DOCS)
    positives = lax.dynamic_slice_in_dim(positive_cols, yl * DOCS, DOCS, 0).T
    scalars = jnp.concatenate([bases, yl.reshape(1).astype(I32)])
    hits, turned = positive_hits(scalars, positives, documents)
    near_grads, near_end, far_grads, far_end, embed_part = second_pass(labels, exps, tops, log_total, hits)

    back = spread(embed_part.reshape(8, DOCS // 8, D))
    own_grad = total(back).astype(BF16)
    embed_grad = everywhere(own_grad).reshape(DOCS, D)

    far_last = jnp.dot(far_end[0], embedding, preferred_element_type=F32).astype(BF16)
    far_last = move(far_last, "core", 2, 1)
    far_rest = jnp.dot(far_grads.reshape(-1, DOCS), embedding, preferred_element_type=F32).astype(BF16)
    far_rest = move(far_rest, "core", 2, 1)
    near_term = jnp.dot(near_end[0], embedding, preferred_element_type=F32)
    last_sum = (near_term + far_last.astype(F32)).astype(BF16)
    near_term = jnp.dot(near_grads.reshape(-1, DOCS), embedding, preferred_element_type=F32)
    rest = (near_term + far_rest.astype(F32)).astype(BF16).reshape(3, TILE, D)
    sums = [rest[0], rest[1], rest[2], last_sum]
    half = TILE // 2
    low_a = move(sums[3][:half], "x", 4, 1)
    high_b = move(sums[3][half:], "x", 4, -1)
    up_hi = move(sums[2][half:], "x", 4, 1)
    down_lo = move(sums[1][:half], "x", 4, -1)
    up_lo = add(sums[2][:half], low_a).astype(BF16)
    down_hi = add(sums[1][half:], high_b).astype(BF16)
    up_lo, down_hi = lax.optimization_barrier((up_lo, down_hi))
    up_lo = move(up_lo, "x", 4, 1)
    down_hi = move(down_hi, "x", 4, -1)

    keep, give = mlp_back(core.reshape(1).astype(I32), embed_grad, down_all, slope, hidden, turned)
    given = move(give, "core", 2, 1)
    both = add(keep, given).astype(BF16)
    mlp = total(lax.all_to_all(both, ("yh", "x", "yl"), 0, 0))

    half = TILE // 2
    lo = (add(sums[0][:half], up_lo) + down_lo.astype(F32)).astype(BF16)
    hi = (add(sums[0][half:], up_hi) + down_hi.astype(F32)).astype(BF16)
    y_sums = [lo[:LAB], lo[LAB:], hi[:LAB], hi[LAB:]]
    half = LAB // 2
    low_a = move(y_sums[3][:half], plane_y, 4, 1)
    high_b = move(y_sums[3][half:], plane_y, 4, -1)
    up = jnp.concatenate([add(y_sums[2][:half], low_a), y_sums[2][half:].astype(F32)], axis=0).astype(BF16)
    down = jnp.concatenate([y_sums[1][:half].astype(F32), add(y_sums[1][half:], high_b)], axis=0).astype(BF16)
    up = move(up, plane_y, 4, 1)
    down = move(down, plane_y, 4, -1)
    label_grad = add(y_sums[0], up) + down.astype(F32)
    return (label_grad, mlp[:, :units], mlp[:, units:].T)


def solution(mesh):
    cut = Mesh(np.asarray(mesh.devices).reshape(2, 4, 2, 8, 2), ("yh", "x", "core", "z", "yl"))
    wide, narrow = ("yh", "x", "core"), ("z", "yl")
    in_specs = (
        P(wide, None),
        P(wide + narrow, None),
        P(wide + narrow),
        P(wide, None),
        P(None, narrow),
        P(narrow, None),
    )
    out_specs = (P(wide + narrow, None), P(wide, narrow), P(narrow, wide))
    return jax.shard_map(step_of, mesh=cut, in_specs=in_specs, out_specs=out_specs, check_vma=False)
```
